512 devices in a mesh: mode: 16 (over x, z_lo), space: 32 (over y, z_hi, core).
Axes of the slice: x: 4, y: 8, z: 8 (z_hi: 2, z_lo: 4; z = z_hi * 4 + z_lo), core: 2. Of those that a mesh axis runs over, the one named last changes fastest.
Arguments:
- modes: bfloat16 [64, 64, 64, 128], P('mode', 'space'), may hold values from -1.25 to 1.25
- regions: int32 [64, 64, 128], P('space'), may hold values from 0 to 7
- stiffness: float32 [8], replicated, may hold values from 0.05 to 4
- nonlinear: float32 [8], replicated, may hold values from 0.5 to 2
- plan: int32 [64, 3], P('mode'), may hold values from 0 to 3
Outputs:
- derivatives: float32 [64, 3, 64, 64, 128], P('mode', None, 'space')
The draws below stay inside these ranges and needn't reach their ends.
All inputs are finite; a program needn't handle non-finite values.
Results may differ from the reference program's by a relative error of at most 0.0003.
Values may be sent and summed in bfloat16 or wider, within the bound.
No kernel may reach another device: no remote copies, remote signals or barrier semaphores. Data moves between devices by JAX's collectives and lax.ppermute only.
A program may use at most 64 MiB of HBM per device.

```python
import math
import jax
import jax.numpy as jnp
from jax import lax

MODES = 64
REGIONS = 8
PARTNERS = 3
ITERS = 3
NY = 64
NZ = 128
NX = 64
N_MODE = 16


def draw_modes(key, part):
    shape = (MODES, NX, NY, NZ)
    layer = jnp.arange(NX, dtype=jnp.int32)
    level = jnp.where(layer < NX // 2, 0.05, 0.22).astype(jnp.float32)[None, :, None, None]
    values = jax.random.normal(key, shape, jnp.float32)
    return jnp.clip(values * level, -1.25, 1.25).astype(jnp.bfloat16)


def draw_regions(key, part):
    layer = jnp.arange(NX, dtype=jnp.int32)[:, None, None]
    lower = jax.random.randint(key, (NX, NY, NZ), 0, REGIONS // 2, dtype=jnp.int32)
    return jnp.where(layer < NX // 2, lower, lower + REGIONS // 2).astype(jnp.int32)


def draw_stiffness(key, part):
    index = jnp.arange(REGIONS, dtype=jnp.int32)
    unit = jax.random.uniform(key, (REGIONS,), jnp.float32)
    softer = 0.05 * jnp.exp2(unit)
    harder = 2.0 * jnp.exp2(unit)
    return jnp.where(index < REGIONS // 2, softer, harder).astype(jnp.float32)


def touch_ends(drawn, own_key, low, largest):
    dims = drawn.shape
    place = [jax.random.randint(jax.random.fold_in(own_key, axis), (), 0, dims[axis]) for axis in range(len(dims))]
    drawn = drawn.at[tuple(place)].set(low)
    longest = dims.index(max(dims))
    place[longest] = (place[longest] + 1) % dims[longest]
    return drawn.at[tuple(place)].set(largest)


def setup_inputs(seed: int = 0) -> dict:
    streams_of = jax.random.split(jax.random.key(seed), 6)
    modes = draw_modes(jax.random.fold_in(streams_of[5], 71), 0)
    regions = draw_regions(jax.random.fold_in(streams_of[5], 71), 0)
    stiffness = draw_stiffness(jax.random.fold_in(streams_of[5], 71), 0)
    nonlinear = jnp.clip(jnp.exp(jax.random.uniform(streams_of[3], (REGIONS,), jnp.float32, math.log(0.5), math.log(2.0))), 0.5, 2.0)
    plan = touch_ends(jax.random.randint(streams_of[4], (MODES, PARTNERS), 0, MODES // N_MODE), jax.random.fold_in(streams_of[4], 1), 0, (MODES // N_MODE) - 1).astype(jnp.int32)
    return {"modes": modes, "regions": regions, "stiffness": stiffness, "nonlinear": nonlinear, "plan": plan}


mass_shift = 0.5


def laplace(field):
    padded = jnp.pad(field, ((1, 1), (1, 1), (1, 1)))
    beside = padded[2:, 1:-1, 1:-1] + padded[:-2, 1:-1, 1:-1]
    beside = beside + padded[1:-1, 2:, 1:-1] + padded[1:-1, :-2, 1:-1]
    beside = beside + padded[1:-1, 1:-1, 2:] + padded[1:-1, 1:-1, :-2]
    return 6.0 * field - beside


def face_weights(coeff):
    padded = jnp.pad(coeff, ((1, 1), (1, 1), (1, 1)))
    lows_x = 0.5 * (coeff + padded[:-2, 1:-1, 1:-1])
    high_x = 0.5 * (coeff + padded[2:, 1:-1, 1:-1])
    lows_y = 0.5 * (coeff + padded[1:-1, :-2, 1:-1])
    high_y = 0.5 * (coeff + padded[1:-1, 2:, 1:-1])
    lows_z = 0.5 * (coeff + padded[1:-1, 1:-1, :-2])
    high_z = 0.5 * (coeff + padded[1:-1, 1:-1, 2:])
    weights = (lows_x, high_x, lows_y, high_y, lows_z, high_z)
    diag = mass_shift + lows_x + high_x + lows_y + high_y + lows_z + high_z
    return weights, diag


def operate(field, weights, diag):
    lows_x, high_x, lows_y, high_y, lows_z, high_z = weights
    padded = jnp.pad(field, ((0, 0), (1, 1), (1, 1), (1, 1)))
    out = diag * field - lows_x * padded[:, :-2, 1:-1, 1:-1] - high_x * padded[:, 2:, 1:-1, 1:-1]
    out = out - lows_y * padded[:, 1:-1, :-2, 1:-1] - high_y * padded[:, 1:-1, 2:, 1:-1]
    out = out - lows_z * padded[:, 1:-1, 1:-1, :-2] - high_z * padded[:, 1:-1, 1:-1, 2:]
    return out


def reference(modes, regions, stiffness, nonlinear, plan):
    coeff = stiffness[regions]
    cubic = nonlinear[regions]
    weights, diag = face_weights(coeff)
    per_block = MODES // N_MODE

    def one_mode(index):
        own = laplace(lax.dynamic_index_in_dim(modes, index, 0, False).astype(jnp.float32))
        block = index // per_block
        steps = jnp.arange(PARTNERS, dtype=jnp.int32)
        partner = ((block - steps) % N_MODE) * per_block + plan[index]
        fields = jnp.take(modes, partner.astype(jnp.int32), axis=0).astype(jnp.float32)
        rhs = jnp.stack([-laplace(cubic * own * laplace(fields[s])) for s in range(PARTNERS)], 0)
        solution = jnp.zeros_like(rhs)
        residual = rhs
        precond = residual / diag
        direction = precond
        norm_now = jnp.sum(residual * precond, axis=(1, 2, 3))
        for step in range(ITERS):
            image = operate(direction, weights, diag)
            alpha = (norm_now / jnp.sum(direction * image, axis=(1, 2, 3)))[:, None, None, None]
            solution = solution + alpha * direction
            residual = residual - alpha * image
            precond = residual / diag
            norm_next = jnp.sum(residual * precond, axis=(1, 2, 3))
            direction = precond + (norm_next / norm_now)[:, None, None, None] * direction
            norm_now = norm_next
        return solution

    return lax.map(one_mode, jnp.arange(MODES, dtype=jnp.int32))
```

```python
import jax
import jax.numpy as jnp
from jax import lax
from jax.experimental import pallas as pl
from jax.experimental.pallas import tpu as pltpu
from jax.sharding import PartitionSpec as P

PARTNERS = 3
MASS = 0.5
WINDOW = 11
MOMENTS = 6


def window_kernel(plan, stiff, cubic, mine, other, edge, first, second, third, sums,
                  wide, lap, coeff, gain, dinv, diag, faces, prod, v0, v1, v2):
    f32 = jnp.float32
    blocks, ny, nz = lap.shape[0] // PARTNERS, wide.shape[2], wide.shape[3]
    space = lax.axis_index("space")
    core = space % 2
    high = (space // 2) % 2
    origin = 4 * high + 2 * core
    stacks = mine.shape[0]

    row = lax.broadcasted_iota(jnp.int32, (ny, nz), 0)
    lane = lax.broadcasted_iota(jnp.int32, (ny, nz), 1)

    def place(ref, slot, at):
        spot = at - origin

        @pl.when(jnp.logical_and(spot >= 0, spot < WINDOW))
        def _():
            def one(m, carry):
                wide[m, spot] = ref[m, slot].astype(f32)
                return carry

            lax.fori_loop(0, stacks, one, 0)

    for ref, q in ((mine, core), (other, 1 - core)):
        for i in range(2):
            place(ref, i, 5 + 4 * high + 2 * q + i)
            place(ref, 2 + i, 5 + 4 * (1 - high) + 2 * q + i)
            place(ref, 4 + i, 1 + 12 * high + 2 * q + i)
    place(edge, 0, 4 * high)

    def shifted(x):
        zero = jnp.zeros_like(x)
        below = jnp.where(row == 0, zero, pltpu.roll(x, 1, 0))
        above = jnp.where(row == ny - 1, zero, pltpu.roll(x, ny - 1, 0))
        left = jnp.where(lane == 0, zero, pltpu.roll(x, 1, 1))
        right = jnp.where(lane == nz - 1, zero, pltpu.roll(x, nz - 1, 1))
        return below, above, left, right

    def rolled(x):
        return pltpu.roll(x, 1, 0), pltpu.roll(x, ny - 1, 0), pltpu.roll(x, 1, 1), pltpu.roll(x, nz - 1, 1)

    for i in range(1, 10):
        label = wide[blocks, i]
        c = jnp.zeros((ny, nz), f32)
        g = jnp.zeros((ny, nz), f32)
        for r in range(stiff.shape[0]):
            hit = label == float(r + 1)
            c = jnp.where(hit, stiff[r], c)
            g = jnp.where(hit, cubic[r], g)
        coeff[i] = c
        gain[i] = g

    for i in range(2, 9):
        c = coeff[i]
        below, above, left, right = shifted(c)
        ws = [0.5 * (c + n) for n in (coeff[i - 1], coeff[i + 1], below, above, left, right)]
        d = MASS + ws[0] + ws[1] + ws[2] + ws[3] + ws[4] + ws[5]
        inv = jnp.where(wide[blocks, i] > 0.5, 1.0 / d, 0.0)
        dinv[i] = inv
        if 5 <= i <= 6:
            diag[i - 5] = d
        if 3 <= i <= 7:
            keep = (None, None, row > 0, row < ny - 1, lane > 0, lane < nz - 1)
            for k in range(6):
                w = ws[k] * inv
                faces[k, i - 3] = w if keep[k] is None else jnp.where(keep[k], w, 0.0)

    def laplace(ref, lead, i):
        x = ref[lead + (i,)]
        below, above, left, right = shifted(x)
        beside = (ref[lead + (i + 1,)] + ref[lead + (i - 1,)]) + (above + below) + (right + left)
        return 6.0 * x - beside

    def lap_one(m, carry):
        src = jnp.where(m < blocks, m, m + 1)
        for i in range(1, 10):
            lap[m, i] = laplace(wide, (src,), i)
        return carry

    lax.fori_loop(0, PARTNERS * blocks, lap_one, 0)

    def image(ref, i, twice):
        x = ref[i]
        below, above, left, right = rolled(x)
        k = i - 3
        out = faces[2, k] * below + faces[3, k] * above + faces[4, k] * left + faces[5, k] * right
        lower = faces[0, k] * ref[i - 1]
        if twice:
            return out + 2.0 * lower
        return out + (lower + faces[1, k] * ref[i + 1])

    mrow = lax.broadcasted_iota(jnp.int32, (8, nz), 0)
    mlane = lax.broadcasted_iota(jnp.int32, (8, nz), 1)

    def field(f, total):
        a = f // PARTNERS
        s = f - PARTNERS * a
        j = s * blocks + plan[a, s]
        for i in range(1, 10):
            prod[i] = gain[i] * lap[a, i] * lap[j, i]
        for i in range(2, 9):
            v0[i] = -laplace(prod, (), i) * dinv[i]
        for i in range(3, 8):
            v1[i] = image(v0, i, False)
        for i in range(4, 7):
            v2[i] = image(v1, i, False)
        parts = [jnp.zeros((8, nz), f32)] * MOMENTS
        for i in (5, 6):
            x0, x1, x2, d = v0[i], v1[i], v2[i], diag[i - 5]
            first[f, i - 5] = x0
            second[f, i - 5] = x1
            third[f, i - 5] = x2
            d1, d2 = d * x1, d * x2
            pairs = (d * x0 * x0, d1 * x0, d1 * x1, d2 * x1, d2 * x2, d2 * image(v2, i, True))
            for k in range(MOMENTS):
                parts[k] = parts[k] + jnp.sum(pairs[k].reshape(ny // 8, 8, nz), axis=0)
        col = jnp.zeros((8, nz), f32)
        for k in range(MOMENTS):
            col = jnp.where(mrow == k, jnp.sum(parts[k], axis=0, keepdims=True), col)
        value = jnp.sum(col, axis=1, keepdims=True)
        return jnp.where(mlane == f, value, total)

    total = lax.fori_loop(0, PARTNERS * blocks, field, jnp.zeros((8, nz), f32))
    for d in range(sums.shape[0]):
        sums[d] = total


def combine_kernel(sums, first, second, third, out):
    m = jnp.sum(sums[...], axis=0)
    mu = [m[k : k + 1] for k in range(MOMENTS)]
    ka = [mu[k] - mu[k + 1] for k in range(MOMENTS - 1)]

    def square(c, form):
        total = None
        for i in range(len(c)):
            for j in range(i, len(c)):
                term = c[i] * c[j] * form[i + j]
                if i != j:
                    term = 2.0 * term
                total = term if total is None else total + term
        return total

    alpha = mu[0] / ka[0]
    x = [alpha, None, None]
    z = [1.0 - alpha, alpha]
    rz = square(z, mu)
    beta = rz / mu[0]
    p = [z[0] + beta, z[1]]
    alpha = rz / square(p, ka)
    x = [x[0] + alpha * p[0], alpha * p[1]]
    z = [z[0] - alpha * p[0], z[1] - alpha * (p[1] - p[0]), alpha * p[1]]
    new = square(z, mu)
    beta = new / rz
    p = [z[0] + beta * p[0], z[1] + beta * p[1], z[2]]
    alpha = new / square(p, ka)
    x = [x[0] + alpha * p[0], x[1] + alpha * p[1], alpha * p[2]]

    lane = lax.broadcasted_iota(jnp.int32, x[0].shape, 1)

    def pick(c, f):
        return jnp.sum(jnp.where(lane == f, c, 0.0), axis=1, keepdims=True)

    for f in range(out.shape[0]):
        c0, c1, c2 = (pick(c, f) for c in x)
        for i in range(out.shape[1]):
            out[f, i] = c0 * first[f, i] + c1 * second[f, i] + c2 * third[f, i]


def shards(modes, regions, stiffness, nonlinear, plan):
    per_block, slabs, ny, nz = modes.shape
    fields = per_block * PARTNERS
    n_mode, n_space = lax.axis_size("mode"), lax.axis_size("space")
    f32 = jnp.float32

    def send(x, to):
        pairs = []
        for m in range(n_mode):
            for s in range(n_space):
                t = to(m, s // 4, (s // 2) % 2, s % 2)
                if t is not None and 0 <= t[1] < n_space // 4:
                    tm, ty, th, tc = t
                    pairs.append((m * n_space + s, (tm % n_mode) * n_space + (ty * 2 + th) * 2 + tc))
        return lax.ppermute(x, ("mode", "space"), pairs)

    labels = (regions + 1).astype(jnp.bfloat16)[None]
    raw = jnp.concatenate([modes, labels], 0)
    near0 = raw
    far0 = send(raw, lambda m, y, h, c: (m, y, 1 - h, c))
    near1 = send(modes, lambda m, y, h, c: (m + 1, y, h, c))
    near2 = send(modes, lambda m, y, h, c: (m + 2, y, h, c))
    far1 = send(modes, lambda m, y, h, c: (m + 1, y, 1 - h, c))
    far2 = send(modes, lambda m, y, h, c: (m + 2, y, 1 - h, c))
    near = jnp.concatenate([near0, near1, near2], 0)
    far = jnp.concatenate([far0, far1, far2], 0)
    edge = send(near[:, 1:], lambda m, y, h, c: (m, y + 1, h, 0) if c == 1 else None)
    along = send(far, lambda m, y, h, c: (m, y + 1 if h == 0 else y - 1, h, c))
    mine = jnp.concatenate([near, far, along], 1)
    other = send(mine, lambda m, y, h, c: (m, y, h, 1 - c))

    vm = pl.BlockSpec(memory_space=pltpu.VMEM)
    sm = pl.BlockSpec(memory_space=pltpu.SMEM)
    slab = (ny, nz)
    whole = jax.ShapeDtypeStruct((fields, slabs, ny, nz), f32)
    first, second, third, sums = pl.pallas_call(
        window_kernel,
        out_shape=(whole, whole, whole, jax.ShapeDtypeStruct((n_space, 8, nz), f32)),
        in_specs=[sm, sm, sm, vm, vm, vm],
        out_specs=(vm, vm, vm, vm),
        scratch_shapes=[
            pltpu.VMEM((fields + 1, WINDOW) + slab, f32),
            pltpu.VMEM((fields, WINDOW) + slab, f32),
            pltpu.VMEM((WINDOW,) + slab, f32),
            pltpu.VMEM((WINDOW,) + slab, f32),
            pltpu.VMEM((WINDOW,) + slab, f32),
            pltpu.VMEM((slabs,) + slab, f32),
            pltpu.VMEM((6, 5) + slab, f32),
            pltpu.VMEM((WINDOW,) + slab, f32),
            pltpu.VMEM((WINDOW,) + slab, f32),
            pltpu.VMEM((WINDOW,) + slab, f32),
            pltpu.VMEM((WINDOW,) + slab, f32),
        ],
        compiler_params=pltpu.CompilerParams(vmem_limit_bytes=24 << 20),
        name="window",
    )(plan, stiffness, nonlinear, mine, other, edge)

    gathered = lax.all_to_all(sums, "space", 0, 0)

    out = pl.pallas_call(
        combine_kernel,
        out_shape=whole,
        in_specs=[vm, vm, vm, vm],
        out_specs=vm,
        name="combine",
    )(gathered, first, second, third)
    return out.reshape((per_block, PARTNERS, slabs, ny, nz))


def solution(mesh):
    return jax.shard_map(
        shards,
        mesh=mesh,
        in_specs=(
            P("mode", "space", None, None),
            P("space", None, None),
            P(),
            P(),
            P("mode", None),
        ),
        out_specs=P("mode", None, "space", None, None),
        check_vma=False,
    )
```

```python
import jax
import jax.numpy as jnp
from jax import lax
from jax.experimental import pallas as pl
from jax.experimental.pallas import tpu as pltpu
from jax.sharding import PartitionSpec as P

PARTNERS = 3
MASS = 0.5
WINDOW = 11
MOMENTS = 6
GROUP = 2
PAD = 8


f32 = jnp.float32


def clear_rims(ref, lead):
    ny = ref.shape[-2] - 2 * PAD
    zero = jnp.zeros((PAD, ref.shape[-1]), f32)
    for i in range(ref.shape[-3]):
        ref[lead + (i, pl.ds(0, PAD))] = zero
        ref[lead + (i, pl.ds(PAD + ny, PAD))] = zero


def fill_window(wide, mine, other, edge, edge_at):
    stacks, ny = mine.shape[0], mine.shape[2]
    space = lax.axis_index("space")
    core = space % 2
    high = (space // 2) % 2
    origin = 4 * high + 2 * core

    def clear(m, carry):
        clear_rims(wide, (m,))
        return carry

    lax.fori_loop(0, stacks, clear, 0)

    def place(ref, slot, at, first):
        spot = at - origin

        @pl.when(jnp.logical_and(spot >= 0, spot < WINDOW))
        def _():
            for m in range(stacks):
                wide[m, spot, pl.ds(PAD, ny)] = ref[first + m, slot].astype(f32)

    for ref, q in ((mine, core), (other, 1 - core)):
        for i in range(2):
            place(ref, i, 5 + 4 * high + 2 * q + i, 0)
            place(ref, 2 + i, 5 + 4 * (1 - high) + 2 * q + i, 0)
            place(ref, 4 + i, 1 + 12 * high + 2 * q + i, 0)
    place(edge, 0, 4 * high, edge_at)


def laplace_at(ref, lead, i, r, lane):
    nz = ref.shape[-1]
    at = PAD + r
    x = ref[lead + (i, pl.ds(at, 8))]
    left = jnp.where(lane == 0, 0.0, pltpu.roll(x, 1, 1))
    right = jnp.where(lane == nz - 1, 0.0, pltpu.roll(x, nz - 1, 1))
    rows = ref[lead + (i, pl.ds(at - 1, 8))] + ref[lead + (i, pl.ds(at + 1, 8))]
    slabs = ref[lead + (i - 1, pl.ds(at, 8))] + ref[lead + (i + 1, pl.ds(at, 8))]
    return 6.0 * x - ((rows + slabs) + (left + right))


def material(wide, label_at, stiff, cubic, gain, dinv, diag, faces):
    ny, nz = gain.shape[-2:]
    row = lax.broadcasted_iota(jnp.int32, (ny, nz), 0)
    lane = lax.broadcasted_iota(jnp.int32, (ny, nz), 1)
    body = pl.ds(PAD, ny)
    for i in range(1, 10):
        label = wide[label_at, i, body]
        c = jnp.zeros((ny, nz), f32)
        g = jnp.zeros((ny, nz), f32)
        for r in range(stiff.shape[0]):
            hit = label == float(r + 1)
            c = jnp.where(hit, stiff[r], c)
            g = jnp.where(hit, cubic[r], g)
        wide[label_at, i, body] = c
        gain[i - 1] = g
    for i in range(2, 9):
        c = wide[label_at, i, body]
        beside = (
            wide[label_at, i - 1, body],
            wide[label_at, i + 1, body],
            wide[label_at, i, pl.ds(PAD - 1, ny)],
            wide[label_at, i, pl.ds(PAD + 1, ny)],
            jnp.where(lane == 0, 0.0, pltpu.roll(c, 1, 1)),
            jnp.where(lane == nz - 1, 0.0, pltpu.roll(c, nz - 1, 1)),
        )
        ws = [0.5 * (c + n) for n in beside]
        d = MASS + ws[0] + ws[1] + ws[2] + ws[3] + ws[4] + ws[5]
        inv = jnp.where(gain[i - 1] > 0.0, 1.0 / d, 0.0)
        dinv[i - 2] = inv
        if 5 <= i <= 6:
            diag[i - 5] = d
        if 3 <= i <= 7:
            for k in range(4):
                faces[k, i - 3] = ws[k] * inv
            faces[4, i - 3] = jnp.where(lane > 0, ws[4] * inv, 0.0)
            faces[5, i - 3] = jnp.where(lane < nz - 1, ws[5] * inv, 0.0)


def krylov(group, lap_own, lap_of, j_of, shared, outs, scratch, total):
    dinv, diag, faces = shared
    first, second, third = outs
    prod, v0, v1, v2 = scratch
    ny, nz = diag.shape[-2:]
    lane = lax.broadcasted_iota(jnp.int32, (8, nz), 1)
    mrow = lax.broadcasted_iota(jnp.int32, (8, nz), 0)
    rows = range(0, ny, 8)

    for t, (a, _, _) in enumerate(group):
        for i in range(1, 10):
            for r in rows:
                at = pl.ds(r, 8)
                prod[t, i, pl.ds(PAD + r, 8)] = lap_own[a, i - 1, at] * lap_of[j_of[t], i - 1, at]
    for i in range(2, 9):
        for r in rows:
            scale = -dinv[i - 2, pl.ds(r, 8)]
            for t in range(len(group)):
                v0[t, i, pl.ds(PAD + r, 8)] = laplace_at(prod, (t,), i, r, lane) * scale

    def image(ref, t, i, r, w, twice):
        at = PAD + r
        x = ref[t, i, pl.ds(at, 8)]
        out = w[2] * ref[t, i, pl.ds(at - 1, 8)] + w[3] * ref[t, i, pl.ds(at + 1, 8)]
        out = out + (w[4] * pltpu.roll(x, 1, 1) + w[5] * pltpu.roll(x, nz - 1, 1))
        lower = w[0] * ref[t, i - 1, pl.ds(at, 8)]
        if twice:
            return out + 2.0 * lower, x
        return out + (lower + w[1] * ref[t, i + 1, pl.ds(at, 8)]), x

    for src, dst, low, top in ((v0, v1, 3, 8), (v1, v2, 4, 7)):
        for i in range(low, top):
            for r in rows:
                w = [faces[k, i - 3, pl.ds(r, 8)] for k in range(6)]
                for t in range(len(group)):
                    dst[t, i, pl.ds(PAD + r, 8)] = image(src, t, i, r, w, False)[0]

    parts = [[jnp.zeros((8, nz), f32)] * MOMENTS for _ in group]
    for i in (5, 6):
        for r in rows:
            w = [faces[k, i - 3, pl.ds(r, 8)] for k in range(6)]
            d = diag[i - 5, pl.ds(r, 8)]
            for t, (_, f, _) in enumerate(group):
                ring, x2 = image(v2, t, i, r, w, True)
                x0, x1 = v0[t, i, pl.ds(PAD + r, 8)], v1[t, i, pl.ds(PAD + r, 8)]
                first[f, i - 5, pl.ds(r, 8)] = x0
                second[f, i - 5, pl.ds(r, 8)] = x1
                third[f, i - 5, pl.ds(r, 8)] = x2
                d0, d1, d2 = d * x0, d * x1, d * x2
                pairs = (d0 * x0, d1 * x0, d1 * x1, d2 * x1, d2 * x2, d2 * ring)
                parts[t] = [p + q for p, q in zip(parts[t], pairs)]
    for t, (_, _, column) in enumerate(group):
        col = jnp.zeros((8, nz), f32)
        for k in range(MOMENTS):
            col = jnp.where(mrow == k, jnp.sum(parts[t][k], axis=0, keepdims=True), col)
        total = jnp.where(lane == column, jnp.sum(col, axis=1, keepdims=True), total)
    return total


def laps(wide, lap, count):
    ny, nz = lap.shape[-2:]
    lane = lax.broadcasted_iota(jnp.int32, (8, nz), 1)

    def one(m, carry):
        for i in range(1, 10):
            for r in range(0, ny, 8):
                lap[m, i - 1, pl.ds(r, 8)] = laplace_at(wide, (m,), i, r, lane)
        return carry

    lax.fori_loop(0, count, one, 0)


def clear_fields(scratch):
    for ref in scratch:
        for t in range(ref.shape[0]):
            clear_rims(ref, (t,))


def own_kernel(plan, stiff, cubic, mine, other, edge,
               first, second, third, lap_own, dinv, diag, faces, moments,
               wide, gain, lap, prod, v0, v1, v2):
    blocks, nz = lap.shape[0], lap.shape[-1]
    scratch = (prod, v0, v1, v2)
    clear_fields(scratch)
    fill_window(wide, mine, other, edge, 0)
    material(wide, blocks, stiff, cubic, gain, dinv, diag, faces)
    laps(wide, lap, blocks)

    def scaled(m, carry):
        for i in range(9):
            lap_own[m, i] = gain[i] * lap[m, i]
        return carry

    lax.fori_loop(0, blocks, scaled, 0)

    def step(h, total):
        group = [(h * GROUP + t, h * GROUP + t, (h * GROUP + t) * PARTNERS) for t in range(GROUP)]
        j_of = [plan[g[0], 0] for g in group]
        return krylov(group, lap_own, lap, j_of, (dinv, diag, faces), (first, second, third), scratch, total)

    moments[...] = lax.fori_loop(0, blocks // GROUP, step, jnp.zeros((8, nz), f32))


def partner_kernel(plan, mine, other, edge, lap_own, dinv, diag, faces, moments,
                   first, second, third, sums,
                   wide, lap, prod, v0, v1, v2):
    blocks = lap_own.shape[0]
    scratch = (prod, v0, v1, v2)
    clear_fields(scratch)
    fill_window(wide, mine, other, edge, blocks + 1)
    laps(wide, lap, lap.shape[0])
    per = blocks // GROUP

    def step(h, total):
        s = 1 + h // per
        b = (h - (s - 1) * per) * GROUP
        group = [(b + t, (s - 1) * blocks + b + t, (b + t) * PARTNERS + s) for t in range(GROUP)]
        j_of = [(s - 1) * blocks + plan[g[0], s] for g in group]
        return krylov(group, lap_own, lap, j_of, (dinv, diag, faces), (first, second, third), scratch, total)

    total = lax.fori_loop(0, (PARTNERS - 1) * per, step, moments[...])
    for d in range(sums.shape[0]):
        sums[d] = total


def combine_kernel(sums, a0, a1, a2, b0, b1, b2, out):
    m = jnp.sum(sums[...], axis=0)
    mu = [m[k : k + 1] for k in range(MOMENTS)]
    ka = [mu[k] - mu[k + 1] for k in range(MOMENTS - 1)]

    def square(c, form):
        total = None
        for i in range(len(c)):
            for j in range(i, len(c)):
                term = c[i] * c[j] * form[i + j]
                if i != j:
                    term = 2.0 * term
                total = term if total is None else total + term
        return total

    alpha = mu[0] / ka[0]
    x = [alpha, None, None]
    z = [1.0 - alpha, alpha]
    rz = square(z, mu)
    beta = rz / mu[0]
    p = [z[0] + beta, z[1]]
    alpha = rz / square(p, ka)
    x = [x[0] + alpha * p[0], alpha * p[1]]
    z = [z[0] - alpha * p[0], z[1] - alpha * (p[1] - p[0]), alpha * p[1]]
    new = square(z, mu)
    beta = new / rz
    p = [z[0] + beta * p[0], z[1] + beta * p[1], z[2]]
    alpha = new / square(p, ka)
    x = [x[0] + alpha * p[0], x[1] + alpha * p[1], alpha * p[2]]

    lane = lax.broadcasted_iota(jnp.int32, x[0].shape, 1)

    def pick(c, f):
        return jnp.sum(jnp.where(lane == f, c, 0.0), axis=1, keepdims=True)

    blocks = a0.shape[0]
    for f in range(out.shape[0]):
        a, s = f // PARTNERS, f % PARTNERS
        basis, at = ((a0, a1, a2), a) if s == 0 else ((b0, b1, b2), (s - 1) * blocks + a)
        c0, c1, c2 = (pick(c, f) for c in x)
        for i in range(out.shape[1]):
            out[f, i] = c0 * basis[0][at, i] + c1 * basis[1][at, i] + c2 * basis[2][at, i]


def shards(modes, regions, stiffness, nonlinear, plan):
    per_block, slabs, ny, nz = modes.shape
    fields = per_block * PARTNERS
    n_mode, n_space = lax.axis_size("mode"), lax.axis_size("space")

    def send(x, to):
        pairs = []
        for m in range(n_mode):
            for s in range(n_space):
                t = to(m, s // 4, (s // 2) % 2, s % 2)
                if t is not None and 0 <= t[1] < n_space // 4:
                    tm, ty, th, tc = t
                    pairs.append((m * n_space + s, (tm % n_mode) * n_space + (ty * 2 + th) * 2 + tc))
        return lax.ppermute(x, ("mode", "space"), pairs)

    def along(m, y, h, c):
        return m, y + 1 if h == 0 else y - 1, h, c

    def partner_core(m, y, h, c):
        return m, y, h, 1 - c

    labels = (regions + 1).astype(jnp.bfloat16)[None]
    raw = jnp.concatenate([modes, labels], 0)
    far0 = send(raw, lambda m, y, h, c: (m, y, 1 - h, c))
    far1 = send(modes, lambda m, y, h, c: (m + 1, y, 1 - h, c))
    far2 = send(modes, lambda m, y, h, c: (m + 2, y, 1 - h, c))
    near1 = send(modes, lambda m, y, h, c: (m + 1, y, h, c))
    near2 = send(modes, lambda m, y, h, c: (m + 2, y, h, c))
    far12 = jnp.concatenate([far1, far2], 0)
    near12 = jnp.concatenate([near1, near2], 0)
    along0 = send(far0, along)
    near = jnp.concatenate([raw, near12], 0)[:, 1:]
    edge = send(near, lambda m, y, h, c: (m, y + 1, h, 0) if c == 1 else None)
    along12 = send(far12, along)
    mine0 = jnp.concatenate([raw, far0, along0], 1)
    mine12 = jnp.concatenate([near12, far12, along12], 1)
    other0 = send(mine0, partner_core)
    other12 = send(mine12, partner_core)

    vm = pl.BlockSpec(memory_space=pltpu.VMEM)
    sm = pl.BlockSpec(memory_space=pltpu.SMEM)
    slab, padded = (ny, nz), (ny + 2 * PAD, nz)

    def array(*shape):
        return jax.ShapeDtypeStruct(shape, f32)

    field_scratch = [pltpu.VMEM((GROUP, WINDOW) + padded, f32) for _ in range(4)]
    vectors = [array(per_block, *(slabs,), *slab)] * 3
    a0, a1, a2, lap_own, dinv, diag, faces, moments = pl.pallas_call(
        own_kernel,
        out_shape=(
            *vectors,
            array(per_block, 9, *slab),
            array(7, *slab),
            array(slabs, *slab),
            array(6, 5, *slab),
            array(8, nz),
        ),
        in_specs=[sm, sm, sm, vm, vm, vm],
        out_specs=(vm,) * 8,
        scratch_shapes=[
            pltpu.VMEM((per_block + 1, WINDOW) + padded, f32),
            pltpu.VMEM((9,) + slab, f32),
            pltpu.VMEM((per_block, 9) + slab, f32),
            *field_scratch,
        ],
        compiler_params=pltpu.CompilerParams(vmem_limit_bytes=24 << 20),
        cost_estimate=pl.CostEstimate(flops=20_000_000, bytes_accessed=8 << 20, transcendentals=0),
        name="own",
    )(plan, stiffness, nonlinear, mine0, other0, edge)

    rest = per_block * (PARTNERS - 1)
    b0, b1, b2, sums = pl.pallas_call(
        partner_kernel,
        out_shape=(*([array(rest, slabs, *slab)] * 3), array(n_space, 8, nz)),
        in_specs=[sm] + [vm] * 8,
        out_specs=(vm,) * 4,
        scratch_shapes=[
            pltpu.VMEM((rest, WINDOW) + padded, f32),
            pltpu.VMEM((rest, 9) + slab, f32),
            *field_scratch,
        ],
        compiler_params=pltpu.CompilerParams(vmem_limit_bytes=24 << 20),
        cost_estimate=pl.CostEstimate(flops=40_000_000, bytes_accessed=16 << 20, transcendentals=0),
        name="partner",
    )(plan, mine12, other12, edge, lap_own, dinv, diag, faces, moments)

    gathered = lax.all_to_all(sums, "space", 0, 0)

    out = pl.pallas_call(
        combine_kernel,
        out_shape=array(fields, slabs, *slab),
        in_specs=[vm] * 7,
        out_specs=vm,
        compiler_params=pltpu.CompilerParams(vmem_limit_bytes=16 << 20),
        name="combine",
    )(gathered, a0, a1, a2, b0, b1, b2)
    return out.reshape((per_block, PARTNERS, slabs, ny, nz))


def solution(mesh):
    return jax.shard_map(
        shards,
        mesh=mesh,
        in_specs=(
            P("mode", "space", None, None),
            P("space", None, None),
            P(),
            P(),
            P("mode", None),
        ),
        out_specs=P("mode", None, "space", None, None),
        check_vma=False,
    )
```

```python
import jax
import jax.numpy as jnp
from jax import lax
from jax.experimental import pallas as pl
from jax.experimental.pallas import tpu as pltpu
from jax.sharding import PartitionSpec as P

PARTNERS = 3
MASS = 0.5
WINDOW = 11
MOMENTS = 6
GROUP = 2
PAD = 8


f32 = jnp.float32


def clear_rims(ref, lead):
    ny = ref.shape[-2] - 2 * PAD
    zero = jnp.zeros((PAD, ref.shape[-1]), f32)
    for i in range(ref.shape[-3]):
        ref[lead + (i, pl.ds(0, PAD))] = zero
        ref[lead + (i, pl.ds(PAD + ny, PAD))] = zero


def position():
    space = lax.axis_index("space")
    core = space % 2
    high = (space // 2) % 2
    return core, high, 4 * high + 2 * core


def clear_window(wide):
    def clear(m, carry):
        clear_rims(wide, (m,))
        return carry

    lax.fori_loop(0, wide.shape[0], clear, 0)


def place(wide, origin, to, ref, slot, at, first, count):
    ny = ref.shape[2]
    spot = at - origin

    @pl.when(jnp.logical_and(spot >= 0, spot < WINDOW))
    def _():
        for m in range(count):
            wide[to + m, spot, pl.ds(PAD, ny)] = ref[first + m, slot].astype(f32)


def laplace_at(ref, lead, i, r, lane):
    nz = ref.shape[-1]
    at = PAD + r
    x = ref[lead + (i, pl.ds(at, 8))]
    left = jnp.where(lane == 0, 0.0, pltpu.roll(x, 1, 1))
    right = jnp.where(lane == nz - 1, 0.0, pltpu.roll(x, nz - 1, 1))
    rows = ref[lead + (i, pl.ds(at - 1, 8))] + ref[lead + (i, pl.ds(at + 1, 8))]
    slabs = ref[lead + (i - 1, pl.ds(at, 8))] + ref[lead + (i + 1, pl.ds(at, 8))]
    return 6.0 * x - ((rows + slabs) + (left + right))


def material(wide, label_at, stiff, cubic, gain, dinv, diag, faces):
    ny, nz = gain.shape[-2:]
    row = lax.broadcasted_iota(jnp.int32, (ny, nz), 0)
    lane = lax.broadcasted_iota(jnp.int32, (ny, nz), 1)
    body = pl.ds(PAD, ny)
    for i in range(1, 10):
        label = wide[label_at, i, body]
        c = jnp.zeros((ny, nz), f32)
        g = jnp.zeros((ny, nz), f32)
        for r in range(stiff.shape[0]):
            hit = label == float(r + 1)
            c = jnp.where(hit, stiff[r], c)
            g = jnp.where(hit, cubic[r], g)
        wide[label_at, i, body] = c
        gain[i - 1] = g
    for i in range(2, 9):
        c = wide[label_at, i, body]
        beside = (
            wide[label_at, i - 1, body],
            wide[label_at, i + 1, body],
            wide[label_at, i, pl.ds(PAD - 1, ny)],
            wide[label_at, i, pl.ds(PAD + 1, ny)],
            jnp.where(lane == 0, 0.0, pltpu.roll(c, 1, 1)),
            jnp.where(lane == nz - 1, 0.0, pltpu.roll(c, nz - 1, 1)),
        )
        ws = [0.5 * (c + n) for n in beside]
        d = MASS + ws[0] + ws[1] + ws[2] + ws[3] + ws[4] + ws[5]
        inv = jnp.where(gain[i - 1] > 0.0, 1.0 / d, 0.0)
        dinv[i - 2] = inv
        if 5 <= i <= 6:
            diag[i - 5] = d
        if 3 <= i <= 7:
            for k in range(4):
                faces[k, i - 3] = ws[k] * inv
            faces[4, i - 3] = jnp.where(lane > 0, ws[4] * inv, 0.0)
            faces[5, i - 3] = jnp.where(lane < nz - 1, ws[5] * inv, 0.0)


def krylov(group, lap_own, lap_of, j_of, shared, outs, scratch, total):
    dinv, diag, faces = shared
    first, second, third = outs
    prod, v0, v1, v2 = scratch
    ny, nz = diag.shape[-2:]
    lane = lax.broadcasted_iota(jnp.int32, (8, nz), 1)
    mrow = lax.broadcasted_iota(jnp.int32, (8, nz), 0)
    rows = range(0, ny, 8)

    for t, (a, _, _) in enumerate(group):
        for i in range(1, 10):
            for r in rows:
                at = pl.ds(r, 8)
                prod[t, i, pl.ds(PAD + r, 8)] = lap_own[a, i - 1, at] * lap_of[j_of[t], i - 1, at]
    for i in range(2, 9):
        for r in rows:
            scale = -dinv[i - 2, pl.ds(r, 8)]
            for t in range(len(group)):
                v0[t, i, pl.ds(PAD + r, 8)] = laplace_at(prod, (t,), i, r, lane) * scale

    def image(ref, t, i, r, w, twice):
        at = PAD + r
        x = ref[t, i, pl.ds(at, 8)]
        out = w[2] * ref[t, i, pl.ds(at - 1, 8)] + w[3] * ref[t, i, pl.ds(at + 1, 8)]
        out = out + (w[4] * pltpu.roll(x, 1, 1) + w[5] * pltpu.roll(x, nz - 1, 1))
        lower = w[0] * ref[t, i - 1, pl.ds(at, 8)]
        if twice:
            return out + 2.0 * lower, x
        return out + (lower + w[1] * ref[t, i + 1, pl.ds(at, 8)]), x

    for src, dst, low, top in ((v0, v1, 3, 8), (v1, v2, 4, 7)):
        for i in range(low, top):
            for r in rows:
                w = [faces[k, i - 3, pl.ds(r, 8)] for k in range(6)]
                for t in range(len(group)):
                    dst[t, i, pl.ds(PAD + r, 8)] = image(src, t, i, r, w, False)[0]

    parts = [[jnp.zeros((8, nz), f32)] * MOMENTS for _ in group]
    for i in (5, 6):
        for r in rows:
            w = [faces[k, i - 3, pl.ds(r, 8)] for k in range(6)]
            d = diag[i - 5, pl.ds(r, 8)]
            for t, (_, f, _) in enumerate(group):
                ring, x2 = image(v2, t, i, r, w, True)
                x0, x1 = v0[t, i, pl.ds(PAD + r, 8)], v1[t, i, pl.ds(PAD + r, 8)]
                first[f, i - 5, pl.ds(r, 8)] = x0
                second[f, i - 5, pl.ds(r, 8)] = x1
                third[f, i - 5, pl.ds(r, 8)] = x2
                d0, d1, d2 = d * x0, d * x1, d * x2
                pairs = (d0 * x0, d1 * x0, d1 * x1, d2 * x1, d2 * x2, d2 * ring)
                parts[t] = [p + q for p, q in zip(parts[t], pairs)]
    for t, (_, _, column) in enumerate(group):
        col = jnp.zeros((8, nz), f32)
        for k in range(MOMENTS):
            col = jnp.where(mrow == k, jnp.sum(parts[t][k], axis=0, keepdims=True), col)
        total = jnp.where(lane == column, jnp.sum(col, axis=1, keepdims=True), total)
    return total


def laps(wide, lap, count):
    ny, nz = lap.shape[-2:]
    lane = lax.broadcasted_iota(jnp.int32, (8, nz), 1)

    def one(m, carry):
        for i in range(1, 10):
            for r in range(0, ny, 8):
                lap[m, i - 1, pl.ds(r, 8)] = laplace_at(wide, (m,), i, r, lane)
        return carry

    lax.fori_loop(0, count, one, 0)


def clear_fields(scratch):
    for ref in scratch:
        for t in range(ref.shape[0]):
            clear_rims(ref, (t,))


def partner_kernel(mine, other, lap, wide):
    count = mine.shape[0]
    core, high, origin = position()
    clear_window(wide)
    for ref, q in ((mine, core), (other, 1 - core)):
        to = q * count
        for k in range(4):
            slab = 2 * q + k if k < 2 else 2 * (1 - q) + k - 2
            place(wide, origin, to, ref, k, 5 + 4 * high + slab, 0, count)
            place(wide, origin, to, ref, 4 + k, 5 + 4 * (1 - high) + slab, 0, count)
            place(wide, origin, to, ref, 8 + k, 1 + 12 * high + slab, 0, count)
        place(wide, origin, to, ref, 12, 4 * high, 0, count)
    laps(wide, lap, lap.shape[0])


def field_kernel(plan, stiff, cubic, mine, other, far, far_other, edge, lap_rest,
                 first, second, third, sums,
                 wide, gain, dinv, diag, faces, lap, lap_own, prod, v0, v1, v2):
    blocks, nz = lap_own.shape[0], lap.shape[-1]
    core, high, origin = position()
    scratch = (prod, v0, v1, v2)
    clear_fields(scratch)
    clear_window(wide)
    stacks = blocks + 1
    for ref, more, q in ((mine, far, core), (other, far_other, 1 - core)):
        for i in range(2):
            place(wide, origin, 0, ref, i, 5 + 4 * high + 2 * q + i, 0, stacks)
            place(wide, origin, 0, more, i, 5 + 4 * (1 - high) + 2 * q + i, 0, stacks)
            place(wide, origin, 0, more, 2 + i, 1 + 12 * high + 2 * q + i, 0, stacks)
    place(wide, origin, 0, edge, 0, 4 * high, 0, stacks)
    material(wide, blocks, stiff, cubic, gain, dinv, diag, faces)
    laps(wide, lap, blocks)

    def scaled(m, carry):
        for i in range(9):
            lap_own[m, i] = gain[i] * lap[m, i]
        return carry

    lax.fori_loop(0, blocks, scaled, 0)

    per = blocks // GROUP
    shared = (dinv, diag, faces)

    def step(lap_of, s, h, total):
        group = [(h * GROUP + t, s * blocks + h * GROUP + t, (h * GROUP + t) * PARTNERS + s) for t in range(GROUP)]
        j_of = [plan[g[0], s] if isinstance(s, int) else (s - 1) * blocks + plan[g[0], s] for g in group]
        return krylov(group, lap_own, lap_of, j_of, shared, (first, second, third), scratch, total)

    total = lax.fori_loop(0, per, lambda h, t: step(lap, 0, h, t), jnp.zeros((8, nz), f32))

    def rest(n, t):
        s = 1 + n // per
        return step(lap_rest, s, n - (s - 1) * per, t)

    total = lax.fori_loop(0, (PARTNERS - 1) * per, rest, total)
    for d in range(sums.shape[0]):
        sums[d] = total


def combine_kernel(sums, v0, v1, v2, out):
    m = jnp.sum(sums[...], axis=0)
    mu = [m[k : k + 1] for k in range(MOMENTS)]
    ka = [mu[k] - mu[k + 1] for k in range(MOMENTS - 1)]

    def square(c, form):
        total = None
        for i in range(len(c)):
            for j in range(i, len(c)):
                term = c[i] * c[j] * form[i + j]
                if i != j:
                    term = 2.0 * term
                total = term if total is None else total + term
        return total

    alpha = mu[0] / ka[0]
    x = [alpha, None, None]
    z = [1.0 - alpha, alpha]
    rz = square(z, mu)
    beta = rz / mu[0]
    p = [z[0] + beta, z[1]]
    alpha = rz / square(p, ka)
    x = [x[0] + alpha * p[0], alpha * p[1]]
    z = [z[0] - alpha * p[0], z[1] - alpha * (p[1] - p[0]), alpha * p[1]]
    new = square(z, mu)
    beta = new / rz
    p = [z[0] + beta * p[0], z[1] + beta * p[1], z[2]]
    alpha = new / square(p, ka)
    x = [x[0] + alpha * p[0], x[1] + alpha * p[1], alpha * p[2]]

    lane = lax.broadcasted_iota(jnp.int32, x[0].shape, 1)

    def pick(c, f):
        return jnp.sum(jnp.where(lane == f, c, 0.0), axis=1, keepdims=True)

    blocks = out.shape[0] // PARTNERS
    for f in range(out.shape[0]):
        at = f % PARTNERS * blocks + f // PARTNERS
        c0, c1, c2 = (pick(c, f) for c in x)
        for i in range(out.shape[1]):
            out[f, i] = c0 * v0[at, i] + c1 * v1[at, i] + c2 * v2[at, i]


def shards(modes, regions, stiffness, nonlinear, plan):
    per_block, slabs, ny, nz = modes.shape
    fields = per_block * PARTNERS
    n_mode, n_space = lax.axis_size("mode"), lax.axis_size("space")

    def send(x, to):
        pairs = []
        for m in range(n_mode):
            for s in range(n_space):
                t = to(m, s // 4, (s // 2) % 2, s % 2)
                if t is not None and 0 <= t[1] < n_space // 4:
                    tm, ty, th, tc = t
                    pairs.append((m * n_space + s, (tm % n_mode) * n_space + (ty * 2 + th) * 2 + tc))
        return lax.ppermute(x, ("mode", "space"), pairs)

    def along(m, y, h, c):
        return m, y + 1 if h == 0 else y - 1, h, c

    def partner_core(m, y, h, c):
        return m, y, h, 1 - c

    core = lax.axis_index("space") % 2
    labels = (regions + 1).astype(jnp.bfloat16)[None]
    raw = jnp.concatenate([modes, labels], 0)
    raw_other = send(raw, partner_core)
    far0 = send(raw, lambda m, y, h, c: (m, y, 1 - h, c))
    chip = jnp.concatenate([raw, raw_other], 1)
    four = chip[:per_block]
    far = send(four, lambda m, y, h, c: (m + 1 + c, y, 1 - h, c))
    near = send(four, lambda m, y, h, c: (m + 1 + c, y, h, c))
    far_along = send(far, along)
    far0_along = send(far0, along)
    last = lax.dynamic_slice_in_dim(jnp.concatenate([chip, near], 0), 3 - 2 * core, 1, 1)
    edge = send(last, lambda m, y, h, c: (m, y + 1, h, c))
    mine = jnp.concatenate([near, far, far_along, edge[per_block + 1 :]], 1)
    other = send(mine, partner_core)
    more = jnp.concatenate([far0, far0_along], 1)
    more_other = send(more, partner_core)

    vm = pl.BlockSpec(memory_space=pltpu.VMEM)
    sm = pl.BlockSpec(memory_space=pltpu.SMEM)
    slab, padded = (ny, nz), (ny + 2 * PAD, nz)

    def array(*shape):
        return jax.ShapeDtypeStruct(shape, f32)

    rest = per_block * (PARTNERS - 1)
    lap_rest = pl.pallas_call(
        partner_kernel,
        out_shape=array(rest, 9, *slab),
        in_specs=[vm] * 2,
        out_specs=vm,
        scratch_shapes=[pltpu.VMEM((rest, WINDOW) + padded, f32)],
        compiler_params=pltpu.CompilerParams(vmem_limit_bytes=20 << 20),
        cost_estimate=pl.CostEstimate(flops=10_000_000, bytes_accessed=8 << 20, transcendentals=0),
        name="partner",
    )(mine, other)

    v0, v1, v2, sums = pl.pallas_call(
        field_kernel,
        out_shape=(*([array(fields, slabs, *slab)] * 3), array(n_space, 8, nz)),
        in_specs=[sm] * 3 + [vm] * 6,
        out_specs=(vm,) * 4,
        scratch_shapes=[
            pltpu.VMEM((per_block + 1, WINDOW) + padded, f32),
            pltpu.VMEM((9,) + slab, f32),
            pltpu.VMEM((7,) + slab, f32),
            pltpu.VMEM((slabs,) + slab, f32),
            pltpu.VMEM((6, 5) + slab, f32),
            pltpu.VMEM((per_block, 9) + slab, f32),
            pltpu.VMEM((per_block, 9) + slab, f32),
            *[pltpu.VMEM((GROUP, WINDOW) + padded, f32) for _ in range(4)],
        ],
        compiler_params=pltpu.CompilerParams(vmem_limit_bytes=24 << 20),
        cost_estimate=pl.CostEstimate(flops=40_000_000, bytes_accessed=16 << 20, transcendentals=0),
        name="fields",
    )(plan, stiffness, nonlinear, raw, raw_other, more, more_other, edge[: per_block + 1], lap_rest)

    gathered = lax.all_to_all(sums, "space", 0, 0)

    out = pl.pallas_call(
        combine_kernel,
        out_shape=array(fields, slabs, *slab),
        in_specs=[vm] * 4,
        out_specs=vm,
        compiler_params=pltpu.CompilerParams(vmem_limit_bytes=16 << 20),
        name="combine",
    )(gathered, v0, v1, v2)
    return out.reshape((per_block, PARTNERS, slabs, ny, nz))


def solution(mesh):
    return jax.shard_map(
        shards,
        mesh=mesh,
        in_specs=(
            P("mode", "space", None, None),
            P("space", None, None),
            P(),
            P(),
            P("mode", None),
        ),
        out_specs=P("mode", None, "space", None, None),
        check_vma=False,
    )
```

```python
import jax
import jax.numpy as jnp
from jax import lax
from jax.experimental import pallas as pl
from jax.experimental.pallas import tpu as pltpu
from jax.sharding import PartitionSpec as P

PARTNERS = 3
MASS = 0.5
WINDOW = 11
MOMENTS = 6
GROUP = 2
PAD = 8


f32 = jnp.float32


def clear_rims(ref, lead):
    ny = ref.shape[-2] - 2 * PAD
    zero = jnp.zeros((PAD, ref.shape[-1]), f32)
    for i in range(ref.shape[-3]):
        ref[lead + (i, pl.ds(0, PAD))] = zero
        ref[lead + (i, pl.ds(PAD + ny, PAD))] = zero


def position():
    space = lax.axis_index("space")
    core = space % 2
    high = (space // 2) % 2
    return core, high, 4 * high + 2 * core


def clear_window(wide):
    def clear(m, carry):
        clear_rims(wide, (m,))
        return carry

    lax.fori_loop(0, wide.shape[0], clear, 0)


def place(wide, origin, to, ref, slot, at, first, count):
    ny = ref.shape[2]
    spot = at - origin

    @pl.when(jnp.logical_and(spot >= 0, spot < WINDOW))
    def _():
        for m in range(count):
            wide[to + m, spot, pl.ds(PAD, ny)] = ref[first + m, slot].astype(f32)


def laplace_at(ref, lead, i, r, lane):
    nz = ref.shape[-1]
    at = PAD + r
    x = ref[lead + (i, pl.ds(at, 8))]
    left = jnp.where(lane == 0, 0.0, pltpu.roll(x, 1, 1))
    right = jnp.where(lane == nz - 1, 0.0, pltpu.roll(x, nz - 1, 1))
    rows = ref[lead + (i, pl.ds(at - 1, 8))] + ref[lead + (i, pl.ds(at + 1, 8))]
    slabs = ref[lead + (i - 1, pl.ds(at, 8))] + ref[lead + (i + 1, pl.ds(at, 8))]
    return 6.0 * x - ((rows + slabs) + (left + right))


def material(wide, label_at, stiff, cubic, gain, dinv, diag, faces):
    ny, nz = gain.shape[-2:]
    row = lax.broadcasted_iota(jnp.int32, (ny, nz), 0)
    lane = lax.broadcasted_iota(jnp.int32, (ny, nz), 1)
    body = pl.ds(PAD, ny)
    for i in range(1, 10):
        label = wide[label_at, i, body]
        c = jnp.zeros((ny, nz), f32)
        g = jnp.zeros((ny, nz), f32)
        for r in range(stiff.shape[0]):
            hit = label == float(r + 1)
            c = jnp.where(hit, stiff[r], c)
            g = jnp.where(hit, cubic[r], g)
        wide[label_at, i, body] = c
        gain[i - 1] = g
    for i in range(2, 9):
        c = wide[label_at, i, body]
        beside = (
            wide[label_at, i - 1, body],
            wide[label_at, i + 1, body],
            wide[label_at, i, pl.ds(PAD - 1, ny)],
            wide[label_at, i, pl.ds(PAD + 1, ny)],
            jnp.where(lane == 0, 0.0, pltpu.roll(c, 1, 1)),
            jnp.where(lane == nz - 1, 0.0, pltpu.roll(c, nz - 1, 1)),
        )
        ws = [0.5 * (c + n) for n in beside]
        d = MASS + ws[0] + ws[1] + ws[2] + ws[3] + ws[4] + ws[5]
        inv = jnp.where(gain[i - 1] > 0.0, 1.0 / d, 0.0)
        dinv[i - 2] = inv
        if 5 <= i <= 6:
            diag[i - 5] = d
        if 3 <= i <= 7:
            for k in range(4):
                faces[k, i - 3] = ws[k] * inv
            faces[4, i - 3] = jnp.where(lane > 0, ws[4] * inv, 0.0)
            faces[5, i - 3] = jnp.where(lane < nz - 1, ws[5] * inv, 0.0)


def krylov(group, lap_own, lap_of, j_of, shared, outs, scratch, total):
    dinv, diag, faces = shared
    first, second, third = outs
    prod, v0, v1, v2 = scratch
    ny, nz = diag.shape[-2:]
    lane = lax.broadcasted_iota(jnp.int32, (8, nz), 1)
    mrow = lax.broadcasted_iota(jnp.int32, (8, nz), 0)
    rows = range(0, ny, 8)

    for t, (a, _, _) in enumerate(group):
        for i in range(1, 10):
            for r in rows:
                at = pl.ds(r, 8)
                prod[t, i, pl.ds(PAD + r, 8)] = lap_own[a, i - 1, at] * lap_of[j_of[t], i - 1, at]
    for i in range(2, 9):
        for r in rows:
            scale = -dinv[i - 2, pl.ds(r, 8)]
            for t in range(len(group)):
                v0[t, i, pl.ds(PAD + r, 8)] = laplace_at(prod, (t,), i, r, lane) * scale

    def image(ref, t, i, r, w, twice):
        at = PAD + r
        x = ref[t, i, pl.ds(at, 8)]
        out = w[2] * ref[t, i, pl.ds(at - 1, 8)] + w[3] * ref[t, i, pl.ds(at + 1, 8)]
        out = out + (w[4] * pltpu.roll(x, 1, 1) + w[5] * pltpu.roll(x, nz - 1, 1))
        lower = w[0] * ref[t, i - 1, pl.ds(at, 8)]
        if twice:
            return out + 2.0 * lower, x
        return out + (lower + w[1] * ref[t, i + 1, pl.ds(at, 8)]), x

    for src, dst, low, top in ((v0, v1, 3, 8), (v1, v2, 4, 7)):
        for i in range(low, top):
            for r in rows:
                w = [faces[k, i - 3, pl.ds(r, 8)] for k in range(6)]
                for t in range(len(group)):
                    dst[t, i, pl.ds(PAD + r, 8)] = image(src, t, i, r, w, False)[0]

    parts = [[jnp.zeros((8, nz), f32)] * MOMENTS for _ in group]
    for i in (5, 6):
        for r in rows:
            w = [faces[k, i - 3, pl.ds(r, 8)] for k in range(6)]
            d = diag[i - 5, pl.ds(r, 8)]
            for t, (_, f, _) in enumerate(group):
                ring, x2 = image(v2, t, i, r, w, True)
                x0, x1 = v0[t, i, pl.ds(PAD + r, 8)], v1[t, i, pl.ds(PAD + r, 8)]
                first[f, i - 5, pl.ds(r, 8)] = x0
                second[f, i - 5, pl.ds(r, 8)] = x1
                third[f, i - 5, pl.ds(r, 8)] = x2
                d0, d1, d2 = d * x0, d * x1, d * x2
                pairs = (d0 * x0, d1 * x0, d1 * x1, d2 * x1, d2 * x2, d2 * ring)
                parts[t] = [p + q for p, q in zip(parts[t], pairs)]
    for t, (_, _, column) in enumerate(group):
        col = jnp.zeros((8, nz), f32)
        for k in range(MOMENTS):
            col = jnp.where(mrow == k, jnp.sum(parts[t][k], axis=0, keepdims=True), col)
        total = jnp.where(lane == column, jnp.sum(col, axis=1, keepdims=True), total)
    return total


def laps(wide, lap, count):
    ny, nz = lap.shape[-2:]
    lane = lax.broadcasted_iota(jnp.int32, (8, nz), 1)

    def one(m, carry):
        for i in range(1, 10):
            for r in range(0, ny, 8):
                lap[m, i - 1, pl.ds(r, 8)] = laplace_at(wide, (m,), i, r, lane)
        return carry

    lax.fori_loop(0, count, one, 0)


def clear_fields(scratch):
    for ref in scratch:
        for t in range(ref.shape[0]):
            clear_rims(ref, (t,))


def pack_kernel(modes, regions, raw):
    blocks = modes.shape[0]
    raw[pl.ds(0, blocks)] = modes[...]
    raw[blocks] = (regions[...] + 1).astype(raw.dtype)


def own_kernel(plan, stiff, cubic, mine, other, far, far_other, edge,
               first, second, third, lap_own, dinv, diag, faces, moments,
               wide, gain, lap, prod, v0, v1, v2):
    blocks, nz = lap.shape[0], lap.shape[-1]
    core, high, origin = position()
    scratch = (prod, v0, v1, v2)
    clear_fields(scratch)
    clear_window(wide)
    stacks = blocks + 1
    for ref, more, q in ((mine, far, core), (other, far_other, 1 - core)):
        for i in range(2):
            place(wide, origin, 0, ref, i, 5 + 4 * high + 2 * q + i, 0, stacks)
            place(wide, origin, 0, more, i, 5 + 4 * (1 - high) + 2 * q + i, 0, stacks)
            place(wide, origin, 0, more, 2 + i, 1 + 12 * high + 2 * q + i, 0, stacks)
    place(wide, origin, 0, edge, 0, 4 * high, 0, stacks)
    material(wide, blocks, stiff, cubic, gain, dinv, diag, faces)
    laps(wide, lap, blocks)

    def scaled(m, carry):
        for i in range(9):
            lap_own[m, i] = gain[i] * lap[m, i]
        return carry

    lax.fori_loop(0, blocks, scaled, 0)

    def step(h, total):
        group = [(h * GROUP + t, h * GROUP + t, (h * GROUP + t) * PARTNERS) for t in range(GROUP)]
        j_of = [plan[g[0], 0] for g in group]
        return krylov(group, lap_own, lap, j_of, (dinv, diag, faces), (first, second, third), scratch, total)

    moments[...] = lax.fori_loop(0, blocks // GROUP, step, jnp.zeros((8, nz), f32))


def partner_kernel(plan, mine, other, lap_own, dinv, diag, faces, moments,
                   first, second, third, sums,
                   wide, lap, prod, v0, v1, v2):
    blocks = mine.shape[0]
    core, high, origin = position()
    scratch = (prod, v0, v1, v2)
    clear_fields(scratch)
    clear_window(wide)
    for ref, q in ((mine, core), (other, 1 - core)):
        to = q * blocks
        for k in range(4):
            slab = 2 * q + k if k < 2 else 2 * (1 - q) + k - 2
            place(wide, origin, to, ref, k, 5 + 4 * high + slab, 0, blocks)
            place(wide, origin, to, ref, 4 + k, 5 + 4 * (1 - high) + slab, 0, blocks)
            place(wide, origin, to, ref, 8 + k, 1 + 12 * high + slab, 0, blocks)
        place(wide, origin, to, ref, 12, 4 * high, 0, blocks)
    laps(wide, lap, lap.shape[0])
    per = blocks // GROUP

    def step(h, total):
        s = 1 + h // per
        b = (h - (s - 1) * per) * GROUP
        group = [(b + t, (s - 1) * blocks + b + t, (b + t) * PARTNERS + s) for t in range(GROUP)]
        j_of = [(s - 1) * blocks + plan[g[0], s] for g in group]
        return krylov(group, lap_own, lap, j_of, (dinv, diag, faces), (first, second, third), scratch, total)

    total = lax.fori_loop(0, (PARTNERS - 1) * per, step, moments[...])
    for d in range(sums.shape[0]):
        sums[d] = total


def combine_kernel(sums, a0, a1, a2, b0, b1, b2, out):
    m = jnp.sum(sums[...], axis=0)
    mu = [m[k : k + 1] for k in range(MOMENTS)]
    ka = [mu[k] - mu[k + 1] for k in range(MOMENTS - 1)]

    def square(c, form):
        total = None
        for i in range(len(c)):
            for j in range(i, len(c)):
                term = c[i] * c[j] * form[i + j]
                if i != j:
                    term = 2.0 * term
                total = term if total is None else total + term
        return total

    alpha = mu[0] / ka[0]
    x = [alpha, None, None]
    z = [1.0 - alpha, alpha]
    rz = square(z, mu)
    beta = rz / mu[0]
    p = [z[0] + beta, z[1]]
    alpha = rz / square(p, ka)
    x = [x[0] + alpha * p[0], alpha * p[1]]
    z = [z[0] - alpha * p[0], z[1] - alpha * (p[1] - p[0]), alpha * p[1]]
    new = square(z, mu)
    beta = new / rz
    p = [z[0] + beta * p[0], z[1] + beta * p[1], z[2]]
    alpha = new / square(p, ka)
    x = [x[0] + alpha * p[0], x[1] + alpha * p[1], alpha * p[2]]

    lane = lax.broadcasted_iota(jnp.int32, x[0].shape, 1)

    def pick(c, f):
        return jnp.sum(jnp.where(lane == f, c, 0.0), axis=1, keepdims=True)

    blocks = a0.shape[0]
    for f in range(out.shape[0]):
        a, s = f // PARTNERS, f % PARTNERS
        basis, at = ((a0, a1, a2), a) if s == 0 else ((b0, b1, b2), (s - 1) * blocks + a)
        c0, c1, c2 = (pick(c, f) for c in x)
        for i in range(out.shape[1]):
            out[f, i] = c0 * basis[0][at, i] + c1 * basis[1][at, i] + c2 * basis[2][at, i]


def shards(modes, regions, stiffness, nonlinear, plan):
    per_block, slabs, ny, nz = modes.shape
    fields = per_block * PARTNERS
    n_mode, n_space = lax.axis_size("mode"), lax.axis_size("space")

    def send(x, to):
        pairs = []
        for m in range(n_mode):
            for s in range(n_space):
                t = to(m, s // 4, (s // 2) % 2, s % 2)
                if t is not None and 0 <= t[1] < n_space // 4:
                    tm, ty, th, tc = t
                    pairs.append((m * n_space + s, (tm % n_mode) * n_space + (ty * 2 + th) * 2 + tc))
        return lax.ppermute(x, ("mode", "space"), pairs)

    def along(m, y, h, c):
        return m, y + 1 if h == 0 else y - 1, h, c

    def partner_core(m, y, h, c):
        return m, y, h, 1 - c

    vm = pl.BlockSpec(memory_space=pltpu.VMEM)
    sm = pl.BlockSpec(memory_space=pltpu.SMEM)
    slab, padded = (ny, nz), (ny + 2 * PAD, nz)

    def array(*shape):
        return jax.ShapeDtypeStruct(shape, f32)

    raw = pl.pallas_call(
        pack_kernel,
        out_shape=jax.ShapeDtypeStruct((per_block + 1, slabs, *slab), modes.dtype),
        in_specs=[vm, vm],
        out_specs=vm,
        compiler_params=pltpu.CompilerParams(vmem_limit_bytes=4 << 20),
        name="pack",
    )(modes, regions)

    odd = lax.axis_index("space") & 1
    raw_other = send(raw, partner_core)
    far0 = send(raw, lambda m, y, h, c: (m, y, 1 - h, c))
    four = jnp.concatenate([raw[:per_block], raw_other[:per_block]], 1)
    far = send(four, lambda m, y, h, c: (m + 1 + c, y, 1 - h, c))
    near = send(four, lambda m, y, h, c: (m + 1 + c, y, h, c))
    edge0 = send(raw[:, 1:], lambda m, y, h, c: (m, y + 1, h, 0) if c == 1 else None)
    far0_along = send(far0, along)
    more = jnp.concatenate([far0, far0_along], 1)
    more_other = send(more, partner_core)

    field_scratch = [pltpu.VMEM((GROUP, WINDOW) + padded, f32) for _ in range(4)]
    vectors = [array(per_block, slabs, *slab)] * 3
    a0, a1, a2, lap_own, dinv, diag, faces, moments = pl.pallas_call(
        own_kernel,
        out_shape=(
            *vectors,
            array(per_block, 9, *slab),
            array(7, *slab),
            array(slabs, *slab),
            array(6, 5, *slab),
            array(8, nz),
        ),
        in_specs=[sm] * 3 + [vm] * 5,
        out_specs=(vm,) * 8,
        scratch_shapes=[
            pltpu.VMEM((per_block + 1, WINDOW) + padded, f32),
            pltpu.VMEM((9,) + slab, f32),
            pltpu.VMEM((per_block, 9) + slab, f32),
            *field_scratch,
        ],
        compiler_params=pltpu.CompilerParams(vmem_limit_bytes=24 << 20),
        cost_estimate=pl.CostEstimate(flops=20_000_000, bytes_accessed=8 << 20, transcendentals=0),
        name="own",
    )(plan, stiffness, nonlinear, raw, raw_other, more, more_other, edge0)

    far_along = send(far, along)
    last = lax.dynamic_slice_in_dim(near, 3 - 2 * odd, 1, 1, allow_negative_indices=False)
    edge = send(last, lambda m, y, h, c: (m, y + 1, h, c))
    mine = jnp.concatenate([near, far, far_along, edge], 1)
    other = send(mine, partner_core)

    rest = per_block * (PARTNERS - 1)
    b0, b1, b2, sums = pl.pallas_call(
        partner_kernel,
        out_shape=(*([array(rest, slabs, *slab)] * 3), array(n_space, 8, nz)),
        in_specs=[sm] + [vm] * 7,
        out_specs=(vm,) * 4,
        scratch_shapes=[
            pltpu.VMEM((rest, WINDOW) + padded, f32),
            pltpu.VMEM((rest, 9) + slab, f32),
            *field_scratch,
        ],
        compiler_params=pltpu.CompilerParams(vmem_limit_bytes=24 << 20),
        cost_estimate=pl.CostEstimate(flops=40_000_000, bytes_accessed=16 << 20, transcendentals=0),
        name="partner",
    )(plan, mine, other, lap_own, dinv, diag, faces, moments)

    gathered = lax.all_to_all(sums, "space", 0, 0)

    out = pl.pallas_call(
        combine_kernel,
        out_shape=array(fields, slabs, *slab),
        in_specs=[vm] * 7,
        out_specs=vm,
        compiler_params=pltpu.CompilerParams(vmem_limit_bytes=16 << 20),
        name="combine",
    )(gathered, a0, a1, a2, b0, b1, b2)
    return out.reshape((per_block, PARTNERS, slabs, ny, nz))


def solution(mesh):
    return jax.shard_map(
        shards,
        mesh=mesh,
        in_specs=(
            P("mode", "space", None, None),
            P("space", None, None),
            P(),
            P(),
            P("mode", None),
        ),
        out_specs=P("mode", None, "space", None, None),
        check_vma=False,
    )
```

```python
import jax
import jax.numpy as jnp
from jax import lax
from jax.experimental import pallas as pl
from jax.experimental.pallas import tpu as pltpu
from jax.sharding import PartitionSpec as P

PARTNERS = 3
MASS = 0.5
WINDOW = 13
OWN = 4
MOMENTS = 6
GROUP = 2
PAD = 8


f32 = jnp.float32


def clear_rims(ref, lead):
    ny = ref.shape[-2] - 2 * PAD
    zero = jnp.zeros((PAD, ref.shape[-1]), f32)
    for i in range(ref.shape[-3]):
        ref[lead + (i, pl.ds(0, PAD))] = zero
        ref[lead + (i, pl.ds(PAD + ny, PAD))] = zero


def position():
    space = lax.axis_index("space")
    return space % 2, (space // 2) % 2


def clear_window(wide):
    def clear(m, carry):
        clear_rims(wide, (m,))
        return carry

    lax.fori_loop(0, wide.shape[0], clear, 0)


def place(wide, ref, slot, at):
    ny = ref.shape[2]
    for m in range(ref.shape[0]):
        wide[m, at, pl.ds(PAD, ny)] = ref[m, slot].astype(f32)


def spots(high):
    return 5, 9 - 8 * high, 1 + 8 * high, 0


def laplace_at(ref, lead, i, r, lane):
    nz = ref.shape[-1]
    at = PAD + r
    x = ref[lead + (i, pl.ds(at, 8))]
    left = jnp.where(lane == 0, 0.0, pltpu.roll(x, 1, 1))
    right = jnp.where(lane == nz - 1, 0.0, pltpu.roll(x, nz - 1, 1))
    rows = ref[lead + (i, pl.ds(at - 1, 8))] + ref[lead + (i, pl.ds(at + 1, 8))]
    slabs = ref[lead + (i - 1, pl.ds(at, 8))] + ref[lead + (i + 1, pl.ds(at, 8))]
    return 6.0 * x - ((rows + slabs) + (left + right))


def material(wide, label_at, stiff, cubic, gain, dinv, diag, faces):
    ny, nz = gain.shape[-2:]
    row = lax.broadcasted_iota(jnp.int32, (ny, nz), 0)
    lane = lax.broadcasted_iota(jnp.int32, (ny, nz), 1)
    body = pl.ds(PAD, ny)
    for i in range(1, 12):
        label = wide[label_at, i, body]
        c = jnp.zeros((ny, nz), f32)
        g = jnp.zeros((ny, nz), f32)
        for r in range(stiff.shape[0]):
            hit = label == float(r + 1)
            c = jnp.where(hit, stiff[r], c)
            g = jnp.where(hit, cubic[r], g)
        wide[label_at, i, body] = c
        gain[i - 1] = g
    for i in range(2, 11):
        c = wide[label_at, i, body]
        beside = (
            wide[label_at, i - 1, body],
            wide[label_at, i + 1, body],
            wide[label_at, i, pl.ds(PAD - 1, ny)],
            wide[label_at, i, pl.ds(PAD + 1, ny)],
            jnp.where(lane == 0, 0.0, pltpu.roll(c, 1, 1)),
            jnp.where(lane == nz - 1, 0.0, pltpu.roll(c, nz - 1, 1)),
        )
        ws = [0.5 * (c + n) for n in beside]
        d = MASS + ws[0] + ws[1] + ws[2] + ws[3] + ws[4] + ws[5]
        inv = jnp.where(gain[i - 1] > 0.0, 1.0 / d, 0.0)
        dinv[i - 2] = inv
        if 5 <= i < 5 + OWN:
            diag[i - 5] = d
        if 3 <= i <= 9:
            for k in range(4):
                faces[k, i - 3] = ws[k] * inv
            faces[4, i - 3] = jnp.where(lane > 0, ws[4] * inv, 0.0)
            faces[5, i - 3] = jnp.where(lane < nz - 1, ws[5] * inv, 0.0)


def krylov(group, lap_own, lap_of, j_of, shared, outs, scratch, total):
    dinv, diag, faces = shared
    keep, give = outs
    prod, v0, v1, v2 = scratch
    ny, nz = diag.shape[-2:]
    lane = lax.broadcasted_iota(jnp.int32, (8, nz), 1)
    mrow = lax.broadcasted_iota(jnp.int32, (8, nz), 0)
    rows = range(0, ny, 8)

    for t, (a, _, _) in enumerate(group):
        for i in range(1, 12):
            for r in rows:
                at = pl.ds(r, 8)
                prod[t, i, pl.ds(PAD + r, 8)] = lap_own[a, i - 1, at] * lap_of[j_of[t], i - 1, at]
    for i in range(2, 11):
        for r in rows:
            scale = -dinv[i - 2, pl.ds(r, 8)]
            for t in range(len(group)):
                v0[t, i, pl.ds(PAD + r, 8)] = laplace_at(prod, (t,), i, r, lane) * scale

    def image(ref, t, i, r, w, twice):
        at = PAD + r
        x = ref[t, i, pl.ds(at, 8)]
        out = w[2] * ref[t, i, pl.ds(at - 1, 8)] + w[3] * ref[t, i, pl.ds(at + 1, 8)]
        out = out + (w[4] * pltpu.roll(x, 1, 1) + w[5] * pltpu.roll(x, nz - 1, 1))
        lower = w[0] * ref[t, i - 1, pl.ds(at, 8)]
        if twice:
            return out + 2.0 * lower, x
        return out + (lower + w[1] * ref[t, i + 1, pl.ds(at, 8)]), x

    for src, dst, low, top in ((v0, v1, 3, 10), (v1, v2, 4, 9)):
        for i in range(low, top):
            for r in rows:
                w = [faces[k, i - 3, pl.ds(r, 8)] for k in range(6)]
                for t in range(len(group)):
                    dst[t, i, pl.ds(PAD + r, 8)] = image(src, t, i, r, w, False)[0]

    parts = [[jnp.zeros((8, nz), f32)] * MOMENTS for _ in group]
    core, _ = position()
    for n in range(OWN):
        half, slab = n // 2, n % 2
        out = keep if half == 0 else give
        i = 5 + 2 * (core if half == 0 else 1 - core) + slab
        for r in rows:
            w = [faces[k, i - 3, pl.ds(r, 8)] for k in range(6)]
            d = diag[i - 5, pl.ds(r, 8)]
            for t, (_, f, _) in enumerate(group):
                ring, x2 = image(v2, t, i, r, w, True)
                x0, x1 = v0[t, i, pl.ds(PAD + r, 8)], v1[t, i, pl.ds(PAD + r, 8)]
                out[0, f, slab, pl.ds(r, 8)] = x0
                out[1, f, slab, pl.ds(r, 8)] = x1
                out[2, f, slab, pl.ds(r, 8)] = x2
                d0, d1, d2 = d * x0, d * x1, d * x2
                pairs = (d0 * x0, d1 * x0, d1 * x1, d2 * x1, d2 * x2, d2 * ring)
                parts[t] = [p + q for p, q in zip(parts[t], pairs)]
    for t, (_, _, column) in enumerate(group):
        col = jnp.zeros((8, nz), f32)
        for k in range(MOMENTS):
            col = jnp.where(mrow == k, jnp.sum(parts[t][k], axis=0, keepdims=True), col)
        total = jnp.where(lane == column, jnp.sum(col, axis=1, keepdims=True), total)
    return total


def laps(wide, lap, count):
    ny, nz = lap.shape[-2:]
    lane = lax.broadcasted_iota(jnp.int32, (8, nz), 1)

    def one(m, carry):
        for i in range(1, 12):
            for r in range(0, ny, 8):
                lap[m, i - 1, pl.ds(r, 8)] = laplace_at(wide, (m,), i, r, lane)
        return carry

    lax.fori_loop(0, count, one, 0)


def clear_fields(scratch):
    for ref in scratch:
        for t in range(ref.shape[0]):
            clear_rims(ref, (t,))


def pack_kernel(modes, regions, raw):
    blocks = modes.shape[0]
    raw[pl.ds(0, blocks)] = modes[...]
    raw[blocks] = (regions[...] + 1).astype(raw.dtype)


def own_kernel(plan, stiff, cubic, mine, other, more, more_other,
               keep, give, lap_own, dinv, diag, faces, moments,
               wide, gain, lap, prod, v0, v1, v2):
    blocks, nz = lap.shape[0], lap.shape[-1]
    core, high = position()
    scratch = (prod, v0, v1, v2)
    clear_fields(scratch)
    clear_window(wide)
    here, there, beyond, edge = spots(high)
    for ref, rest, q in ((mine, more, core), (other, more_other, 1 - core)):
        for i in range(2):
            place(wide, ref, i, here + 2 * q + i)
            place(wide, rest, i, there + 2 * q + i)
            place(wide, rest, 2 + i, beyond + 2 * q + i)

        @pl.when(q == 0)
        def _():
            place(wide, rest, 4, edge)

    material(wide, blocks, stiff, cubic, gain, dinv, diag, faces)
    laps(wide, lap, blocks)

    def scaled(m, carry):
        for i in range(gain.shape[0]):
            lap_own[m, i] = gain[i] * lap[m, i]
        return carry

    lax.fori_loop(0, blocks, scaled, 0)
    group = [(GROUP * core + t, t, (GROUP * core + t) * PARTNERS) for t in range(GROUP)]
    j_of = [plan[g[0], 0] for g in group]
    moments[...] = krylov(
        group, lap_own, lap, j_of, (dinv, diag, faces), (keep, give), scratch, jnp.zeros((8, nz), f32)
    )


def partner_kernel(plan, near, far, along, edge, lap_own, dinv, diag, faces, moments, keep_own, give_own,
                   keep, give, sums,
                   wide, lap, prod, v0, v1, v2):
    blocks = near.shape[0]
    core, high = position()
    scratch = (prod, v0, v1, v2)
    clear_fields(scratch)
    clear_window(wide)
    for ref, first in zip((near, far, along), spots(high)):
        for k in range(OWN):
            place(wide, ref, k, first + (2 * core + k if k < 2 else 2 * (1 - core) + k - 2))
    place(wide, edge, 0, 0)
    for k in range(3):
        keep[k, pl.ds(0, GROUP)] = keep_own[k]
        give[k, pl.ds(0, GROUP)] = give_own[k]
    laps(wide, lap, blocks)
    s = 1 + core

    def step(h, total):
        b = h * GROUP
        group = [(b + t, GROUP + b + t, (b + t) * PARTNERS + s) for t in range(GROUP)]
        j_of = [plan[g[0], s] for g in group]
        return krylov(group, lap_own, lap, j_of, (dinv, diag, faces), (keep, give), scratch, total)

    total = lax.fori_loop(0, blocks // GROUP, step, moments[...])
    for d in range(sums.shape[0]):
        sums[d] = total


def combine_kernel(sums, keep, got, out):
    m = jnp.sum(sums[...], axis=0)
    mu = [m[k : k + 1] for k in range(MOMENTS)]
    ka = [mu[k] - mu[k + 1] for k in range(MOMENTS - 1)]

    def square(c, form):
        total = None
        for i in range(len(c)):
            for j in range(i, len(c)):
                term = c[i] * c[j] * form[i + j]
                if i != j:
                    term = 2.0 * term
                total = term if total is None else total + term
        return total

    alpha = mu[0] / ka[0]
    x = [alpha, None, None]
    z = [1.0 - alpha, alpha]
    rz = square(z, mu)
    beta = rz / mu[0]
    p = [z[0] + beta, z[1]]
    alpha = rz / square(p, ka)
    x = [x[0] + alpha * p[0], alpha * p[1]]
    z = [z[0] - alpha * p[0], z[1] - alpha * (p[1] - p[0]), alpha * p[1]]
    new = square(z, mu)
    beta = new / rz
    p = [z[0] + beta * p[0], z[1] + beta * p[1], z[2]]
    alpha = new / square(p, ka)
    x = [x[0] + alpha * p[0], x[1] + alpha * p[1], alpha * p[2]]

    lane = lax.broadcasted_iota(jnp.int32, x[0].shape, 1)

    def pick(c, f):
        return jnp.sum(jnp.where(lane == f, c, 0.0), axis=1, keepdims=True)

    core, _ = position()
    for basis, q in ((keep, core), (got, 1 - core)):
        for n in range(basis.shape[1]):
            f = (GROUP * q + n) * PARTNERS if n < GROUP else (n - GROUP) * PARTNERS + 1 + q
            c0, c1, c2 = (pick(c, f) for c in x)
            for i in range(out.shape[1]):
                out[f, i] = c0 * basis[0, n, i] + c1 * basis[1, n, i] + c2 * basis[2, n, i]


def shards(modes, regions, stiffness, nonlinear, plan):
    per_block, slabs, ny, nz = modes.shape
    fields = per_block * PARTNERS
    n_mode, n_space = lax.axis_size("mode"), lax.axis_size("space")

    def send(x, to):
        pairs = []
        for m in range(n_mode):
            for s in range(n_space):
                t = to(m, s // 4, (s // 2) % 2, s % 2)
                if t is not None and 0 <= t[1] < n_space // 4:
                    tm, ty, th, tc = t
                    pairs.append((m * n_space + s, (tm % n_mode) * n_space + (ty * 2 + th) * 2 + tc))
        return lax.ppermute(x, ("mode", "space"), pairs)

    def along(m, y, h, c):
        return m, y + 1 if h == 0 else y - 1, h, c

    def partner_core(m, y, h, c):
        return m, y, h, 1 - c

    vm = pl.BlockSpec(memory_space=pltpu.VMEM)
    sm = pl.BlockSpec(memory_space=pltpu.SMEM)
    slab, padded = (ny, nz), (ny + 2 * PAD, nz)

    def array(*shape):
        return jax.ShapeDtypeStruct(shape, f32)

    raw = pl.pallas_call(
        pack_kernel,
        out_shape=jax.ShapeDtypeStruct((per_block + 1, slabs, *slab), modes.dtype),
        in_specs=[vm, vm],
        out_specs=vm,
        compiler_params=pltpu.CompilerParams(vmem_limit_bytes=4 << 20),
        name="pack",
    )(modes, regions)

    odd = lax.axis_index("space") & 1
    raw_other = send(raw, partner_core)
    far0 = send(raw, lambda m, y, h, c: (m, y, 1 - h, c))
    four = jnp.concatenate([raw[:per_block], raw_other[:per_block]], 1)
    far = send(four, lambda m, y, h, c: (m + 1 + c, y, 1 - h, c))
    near = send(four, lambda m, y, h, c: (m + 1 + c, y, h, c))
    edge0 = send(raw[:, 1:], lambda m, y, h, c: (m, y + 1, h, 0) if c == 1 else None)
    far0_along = send(far0, along)
    more = jnp.concatenate([far0, far0_along, edge0], 1)
    more_other = send(more, partner_core)

    field_scratch = [pltpu.VMEM((GROUP, WINDOW) + padded, f32) for _ in range(4)]
    basis = array(3, GROUP, slabs, *slab)
    keep_own, give_own, lap_own, dinv, diag, faces, moments = pl.pallas_call(
        own_kernel,
        out_shape=(
            basis,
            basis,
            array(per_block, WINDOW - 2, *slab),
            array(WINDOW - 4, *slab),
            array(OWN, *slab),
            array(6, WINDOW - 6, *slab),
            array(8, nz),
        ),
        in_specs=[sm] * 3 + [vm] * 4,
        out_specs=(vm,) * 7,
        scratch_shapes=[
            pltpu.VMEM((per_block + 1, WINDOW) + padded, f32),
            pltpu.VMEM((WINDOW - 2,) + slab, f32),
            pltpu.VMEM((per_block, WINDOW - 2) + slab, f32),
            *field_scratch,
        ],
        compiler_params=pltpu.CompilerParams(vmem_limit_bytes=24 << 20),
        cost_estimate=pl.CostEstimate(flops=20_000_000, bytes_accessed=8 << 20, transcendentals=0),
        name="own",
    )(plan, stiffness, nonlinear, raw, raw_other, more, more_other)

    far_along = send(far, along)
    last = lax.dynamic_slice_in_dim(near, 3 - 2 * odd, 1, 1, allow_negative_indices=False)
    edge = send(last, lambda m, y, h, c: (m, y + 1, h, c))

    basis = array(3, GROUP + per_block, slabs, *slab)
    keep, give, sums = pl.pallas_call(
        partner_kernel,
        out_shape=(basis, basis, array(n_space, 8, nz)),
        in_specs=[sm] + [vm] * 11,
        out_specs=(vm,) * 3,
        scratch_shapes=[
            pltpu.VMEM((per_block, WINDOW) + padded, f32),
            pltpu.VMEM((per_block, WINDOW - 2) + slab, f32),
            *field_scratch,
        ],
        compiler_params=pltpu.CompilerParams(vmem_limit_bytes=24 << 20),
        cost_estimate=pl.CostEstimate(flops=40_000_000, bytes_accessed=16 << 20, transcendentals=0),
        name="partner",
    )(plan, near, far, far_along, edge, lap_own, dinv, diag, faces, moments, keep_own, give_own)

    got = send(give, partner_core)
    gathered = lax.all_to_all(sums, "space", 0, 0)

    out = pl.pallas_call(
        combine_kernel,
        out_shape=array(fields, slabs, *slab),
        in_specs=[vm] * 3,
        out_specs=vm,
        compiler_params=pltpu.CompilerParams(vmem_limit_bytes=16 << 20),
        name="combine",
    )(gathered, keep, got)
    return out.reshape((per_block, PARTNERS, slabs, ny, nz))


def solution(mesh):
    return jax.shard_map(
        shards,
        mesh=mesh,
        in_specs=(
            P("mode", "space", None, None),
            P("space", None, None),
            P(),
            P(),
            P("mode", None),
        ),
        out_specs=P("mode", None, "space", None, None),
        check_vma=False,
    )
```

```python
import jax
import jax.numpy as jnp
from jax import lax
from jax.experimental import pallas as pl
from jax.experimental.pallas import tpu as pltpu
from jax.sharding import PartitionSpec as P

PARTNERS = 3
MASS = 0.5
WINDOW = 13
OWN = 4
MOMENTS = 6
GROUP = 2
PAD = 8


f32 = jnp.float32


def clear_rims(ref, lead):
    ny = ref.shape[-2] - 2 * PAD
    zero = jnp.zeros((PAD, ref.shape[-1]), f32)
    for i in range(ref.shape[-3]):
        ref[lead + (i, pl.ds(0, PAD))] = zero
        ref[lead + (i, pl.ds(PAD + ny, PAD))] = zero


def position():
    space = lax.axis_index("space")
    return space % 2, (space // 2) % 2


def clear_window(wide):
    def clear(m, carry):
        clear_rims(wide, (m,))
        return carry

    lax.fori_loop(0, wide.shape[0], clear, 0)


def place(wide, exact, ref, slot, at):
    ny = ref.shape[2]
    for m in range(ref.shape[0]):
        wide[m, at, pl.ds(PAD, ny)] = ref[m, slot].astype(f32)
    for m in range(exact.shape[0]):
        exact[m, at] = ref[m, slot]


def spots(high):
    return 5, 9 - 8 * high, 1 + 8 * high, 0


def laplace_at(ref, lead, i, r, lane):
    nz = ref.shape[-1]
    at = PAD + r
    x = ref[lead + (i, pl.ds(at, 8))]
    left = jnp.where(lane == 0, 0.0, pltpu.roll(x, 1, 1))
    right = jnp.where(lane == nz - 1, 0.0, pltpu.roll(x, nz - 1, 1))
    rows = ref[lead + (i, pl.ds(at - 1, 8))] + ref[lead + (i, pl.ds(at + 1, 8))]
    slabs = ref[lead + (i - 1, pl.ds(at, 8))] + ref[lead + (i + 1, pl.ds(at, 8))]
    return 6.0 * x - ((rows + slabs) + (left + right))


def material(wide, label_at, stiff, cubic, gain, dinv, diag, faces):
    ny, nz = gain.shape[-2:]
    row = lax.broadcasted_iota(jnp.int32, (ny, nz), 0)
    lane = lax.broadcasted_iota(jnp.int32, (ny, nz), 1)
    body = pl.ds(PAD, ny)
    for i in range(1, 12):
        label = wide[label_at, i, body]
        c = jnp.zeros((ny, nz), f32)
        g = jnp.zeros((ny, nz), f32)
        for r in range(stiff.shape[0]):
            hit = label == float(r + 1)
            c = jnp.where(hit, stiff[r], c)
            g = jnp.where(hit, cubic[r], g)
        wide[label_at, i, body] = c
        gain[i - 1] = g
    for i in range(2, 11):
        c = wide[label_at, i, body]
        beside = (
            wide[label_at, i - 1, body],
            wide[label_at, i + 1, body],
            wide[label_at, i, pl.ds(PAD - 1, ny)],
            wide[label_at, i, pl.ds(PAD + 1, ny)],
            jnp.where(lane == 0, 0.0, pltpu.roll(c, 1, 1)),
            jnp.where(lane == nz - 1, 0.0, pltpu.roll(c, nz - 1, 1)),
        )
        ws = [0.5 * (c + n) for n in beside]
        d = MASS + ws[0] + ws[1] + ws[2] + ws[3] + ws[4] + ws[5]
        inv = jnp.where(gain[i - 1] > 0.0, 1.0 / d, 0.0)
        dinv[i - 2] = inv
        if 5 <= i < 5 + OWN:
            diag[i - 5] = d
        if 3 <= i <= 9:
            for k in range(4):
                faces[k, i - 3] = ws[k] * inv
            faces[4, i - 3] = jnp.where(lane > 0, ws[4] * inv, 0.0)
            faces[5, i - 3] = jnp.where(lane < nz - 1, ws[5] * inv, 0.0)


def krylov(group, lap_own, lap_of, j_of, shared, outs, scratch, total):
    dinv, diag, faces = shared
    keep, give = outs
    prod, v0, v1, v2 = scratch
    ny, nz = diag.shape[-2:]
    lane = lax.broadcasted_iota(jnp.int32, (8, nz), 1)
    mrow = lax.broadcasted_iota(jnp.int32, (8, nz), 0)
    rows = range(0, ny, 8)

    for t, (a, _, _) in enumerate(group):
        for i in range(1, 12):
            for r in rows:
                at = pl.ds(r, 8)
                prod[t, i, pl.ds(PAD + r, 8)] = lap_own[a, i - 1, at] * lap_of[j_of[t], i - 1, at]
    for i in range(2, 11):
        for r in rows:
            scale = -dinv[i - 2, pl.ds(r, 8)]
            for t in range(len(group)):
                v0[t, i, pl.ds(PAD + r, 8)] = laplace_at(prod, (t,), i, r, lane) * scale

    def image(ref, t, i, r, w):
        at = PAD + r
        x = ref[t, i, pl.ds(at, 8)]
        out = w[2] * ref[t, i, pl.ds(at - 1, 8)] + w[3] * ref[t, i, pl.ds(at + 1, 8)]
        out = out + (w[4] * pltpu.roll(x, 1, 1) + w[5] * pltpu.roll(x, nz - 1, 1))
        return out + (w[0] * ref[t, i - 1, pl.ds(at, 8)] + w[1] * ref[t, i + 1, pl.ds(at, 8)])

    def lower(ref, t, i, r, w):
        at = PAD + r
        x = ref[t, i, pl.ds(at, 8)]
        out = w[0] * ref[t, i - 1, pl.ds(at, 8)] + w[1] * ref[t, i, pl.ds(at - 1, 8)]
        return 2.0 * (out + w[2] * pltpu.roll(x, 1, 1)), x

    for src, dst, low, top in ((v0, v1, 3, 10), (v1, v2, 4, 9)):
        for i in range(low, top):
            for r in rows:
                w = [faces[k, i - 3, pl.ds(r, 8)] for k in range(6)]
                for t in range(len(group)):
                    dst[t, i, pl.ds(PAD + r, 8)] = image(src, t, i, r, w)

    parts = [[jnp.zeros((8, nz), f32)] * MOMENTS for _ in group]
    core, _ = position()
    for n in range(OWN):
        half, slab = n // 2, n % 2
        out = keep if half == 0 else give
        i = 5 + 2 * (core if half == 0 else 1 - core) + slab
        for r in rows:
            w = [faces[k, i - 3, pl.ds(r, 8)] for k in (0, 2, 4)]
            d = diag[i - 5, pl.ds(r, 8)]
            for t, (_, f, _) in enumerate(group):
                ring, x2 = lower(v2, t, i, r, w)
                x0, x1 = v0[t, i, pl.ds(PAD + r, 8)], v1[t, i, pl.ds(PAD + r, 8)]
                out[0, f, slab, pl.ds(r, 8)] = x0
                out[1, f, slab, pl.ds(r, 8)] = x1
                out[2, f, slab, pl.ds(r, 8)] = x2
                d0, d1, d2 = d * x0, d * x1, d * x2
                pairs = (d0 * x0, d1 * x0, d1 * x1, d2 * x1, d2 * x2, d2 * ring)
                parts[t] = [p + q for p, q in zip(parts[t], pairs)]
    for t, (_, _, column) in enumerate(group):
        col = jnp.zeros((8, nz), f32)
        for k in range(MOMENTS):
            col = jnp.where(mrow == k, jnp.sum(parts[t][k], axis=0, keepdims=True), col)
        total = jnp.where(lane == column, jnp.sum(col, axis=1, keepdims=True), total)
    return total


def laps(wide, exact, lap):
    count, places, ny, nz = lap.shape
    r = lax.broadcasted_iota(jnp.int32, (nz, nz), 0)
    c = lax.broadcasted_iota(jnp.int32, (nz, nz), 1)
    beside = jnp.where(jnp.abs(r - c) == 1, -1.0, 0.0)
    line = jnp.where(r == c, 6.0, beside).astype(exact.dtype)

    def one(m, carry):
        rows = exact[m, pl.ds(1, places)].reshape(places * ny, nz)
        lap[m] = jnp.dot(rows, line, preferred_element_type=f32).reshape(places, ny, nz)
        for i in range(1, places + 1):
            for r in range(0, ny, 8):
                at = PAD + r
                beside = wide[m, i, pl.ds(at - 1, 8)] + wide[m, i, pl.ds(at + 1, 8)]
                slabs = wide[m, i - 1, pl.ds(at, 8)] + wide[m, i + 1, pl.ds(at, 8)]
                lap[m, i - 1, pl.ds(r, 8)] = lap[m, i - 1, pl.ds(r, 8)] - (beside + slabs)
        return carry

    lax.fori_loop(0, count, one, 0)


def clear_fields(scratch):
    for ref in scratch:
        for t in range(ref.shape[0]):
            clear_rims(ref, (t,))


def pack_kernel(modes, labels, raw):
    blocks = modes.shape[0]
    raw[pl.ds(0, blocks)] = modes[...]
    raw[blocks] = labels[...]


def own_kernel(plan, stiff, cubic, mine, other, more, more_other,
               keep, give, lap_own, dinv, diag, faces, moments,
               wide, exact, gain, lap, prod, v0, v1, v2):
    blocks, nz = lap.shape[0], lap.shape[-1]
    core, high = position()
    scratch = (prod, v0, v1, v2)
    clear_fields(scratch)
    clear_window(wide)
    here, there, beyond, edge = spots(high)
    for ref, rest, q in ((mine, more, core), (other, more_other, 1 - core)):
        for i in range(2):
            place(wide, exact, ref, i, here + 2 * q + i)
            place(wide, exact, rest, i, there + 2 * q + i)
            place(wide, exact, rest, 2 + i, beyond + 2 * q + i)

        @pl.when(q == 0)
        def _():
            place(wide, exact, rest, 4, edge)

    material(wide, blocks, stiff, cubic, gain, dinv, diag, faces)
    laps(wide, exact, lap)

    def scaled(m, carry):
        for i in range(gain.shape[0]):
            lap_own[m, i] = gain[i] * lap[m, i]
        return carry

    lax.fori_loop(0, blocks, scaled, 0)
    group = [(GROUP * core + t, t, (GROUP * core + t) * PARTNERS) for t in range(GROUP)]
    j_of = [plan[g[0], 0] for g in group]
    moments[...] = krylov(
        group, lap_own, lap, j_of, (dinv, diag, faces), (keep, give), scratch, jnp.zeros((8, nz), f32)
    )


def partner_kernel(plan, near, far, along, edge, lap_own, dinv, diag, faces, moments, keep_own, give_own,
                   keep, give, sums,
                   wide, exact, lap, prod, v0, v1, v2):
    blocks = near.shape[0]
    core, high = position()
    scratch = (prod, v0, v1, v2)
    clear_fields(scratch)
    clear_window(wide)
    for ref, first in zip((near, far, along), spots(high)):
        for k in range(OWN):
            place(wide, exact, ref, k, first + (2 * core + k if k < 2 else 2 * (1 - core) + k - 2))
    place(wide, exact, edge, 0, 0)
    for k in range(3):
        keep[k, pl.ds(0, GROUP)] = keep_own[k]
        give[k, pl.ds(0, GROUP)] = give_own[k]
    laps(wide, exact, lap)
    s = 1 + core

    def step(h, total):
        b = h * GROUP
        group = [(b + t, GROUP + b + t, (b + t) * PARTNERS + s) for t in range(GROUP)]
        j_of = [plan[g[0], s] for g in group]
        return krylov(group, lap_own, lap, j_of, (dinv, diag, faces), (keep, give), scratch, total)

    total = lax.fori_loop(0, blocks // GROUP, step, moments[...])
    for d in range(sums.shape[0]):
        sums[d] = total


def combine_kernel(sums, keep, got, out):
    m = jnp.sum(sums[...], axis=0)
    mu = [m[k : k + 1] for k in range(MOMENTS)]
    ka = [mu[k] - mu[k + 1] for k in range(MOMENTS - 1)]

    def square(c, form):
        total = None
        for i in range(len(c)):
            for j in range(i, len(c)):
                term = c[i] * c[j] * form[i + j]
                if i != j:
                    term = 2.0 * term
                total = term if total is None else total + term
        return total

    alpha = mu[0] / ka[0]
    x = [alpha, None, None]
    z = [1.0 - alpha, alpha]
    rz = square(z, mu)
    beta = rz / mu[0]
    p = [z[0] + beta, z[1]]
    alpha = rz / square(p, ka)
    x = [x[0] + alpha * p[0], alpha * p[1]]
    z = [z[0] - alpha * p[0], z[1] - alpha * (p[1] - p[0]), alpha * p[1]]
    new = square(z, mu)
    beta = new / rz
    p = [z[0] + beta * p[0], z[1] + beta * p[1], z[2]]
    alpha = new / square(p, ka)
    x = [x[0] + alpha * p[0], x[1] + alpha * p[1], alpha * p[2]]

    lane = lax.broadcasted_iota(jnp.int32, x[0].shape, 1)

    def pick(c, f):
        return jnp.sum(jnp.where(lane == f, c, 0.0), axis=1, keepdims=True)

    core, _ = position()
    for basis, q in ((keep, core), (got, 1 - core)):
        for n in range(basis.shape[1]):
            f = (GROUP * q + n) * PARTNERS if n < GROUP else (n - GROUP) * PARTNERS + 1 + q
            c0, c1, c2 = (pick(c, f) for c in x)
            for i in range(out.shape[1]):
                out[f, i] = c0 * basis[0, n, i] + c1 * basis[1, n, i] + c2 * basis[2, n, i]


def shards(modes, regions, stiffness, nonlinear, plan):
    per_block, slabs, ny, nz = modes.shape
    fields = per_block * PARTNERS
    n_mode, n_space = lax.axis_size("mode"), lax.axis_size("space")

    def send(x, to):
        pairs = []
        for m in range(n_mode):
            for s in range(n_space):
                t = to(m, s // 4, (s // 2) % 2, s % 2)
                if t is not None and 0 <= t[1] < n_space // 4:
                    tm, ty, th, tc = t
                    pairs.append((m * n_space + s, (tm % n_mode) * n_space + (ty * 2 + th) * 2 + tc))
        return lax.ppermute(x, ("mode", "space"), pairs)

    def along(m, y, h, c):
        return m, y + 1 if h == 0 else y - 1, h, c

    def partner_core(m, y, h, c):
        return m, y, h, 1 - c

    vm = pl.BlockSpec(memory_space=pltpu.VMEM)
    sm = pl.BlockSpec(memory_space=pltpu.SMEM)
    slab, padded = (ny, nz), (ny + 2 * PAD, nz)

    def array(*shape):
        return jax.ShapeDtypeStruct(shape, f32)

    raw = pl.pallas_call(
        pack_kernel,
        out_shape=jax.ShapeDtypeStruct((per_block + 1, slabs, *slab), modes.dtype),
        in_specs=[vm, vm],
        out_specs=vm,
        compiler_params=pltpu.CompilerParams(vmem_limit_bytes=4 << 20),
        name="pack",
    )(modes, (regions + 1).astype(modes.dtype))

    odd = lax.axis_index("space") & 1
    raw_other = send(raw, partner_core)
    far0 = send(raw, lambda m, y, h, c: (m, y, 1 - h, c))
    four = jnp.concatenate([raw[:per_block], raw_other[:per_block]], 1)
    far = send(four, lambda m, y, h, c: (m + 1 + c, y, 1 - h, c))
    near = send(four, lambda m, y, h, c: (m + 1 + c, y, h, c))
    edge0 = send(raw[:, 1:], lambda m, y, h, c: (m, y + 1, h, 0) if c == 1 else None)
    far0_along = send(far0, along)
    more = jnp.concatenate([far0, far0_along, edge0], 1)
    more_other = send(more, partner_core)

    field_scratch = [pltpu.VMEM((GROUP, WINDOW) + padded, f32) for _ in range(4)]
    basis = array(3, GROUP, slabs, *slab)
    keep_own, give_own, lap_own, dinv, diag, faces, moments = pl.pallas_call(
        own_kernel,
        out_shape=(
            basis,
            basis,
            array(per_block, WINDOW - 2, *slab),
            array(WINDOW - 4, *slab),
            array(OWN, *slab),
            array(6, WINDOW - 6, *slab),
            array(8, nz),
        ),
        in_specs=[sm] * 3 + [vm] * 4,
        out_specs=(vm,) * 7,
        scratch_shapes=[
            pltpu.VMEM((per_block + 1, WINDOW) + padded, f32),
            pltpu.VMEM((per_block, WINDOW) + slab, modes.dtype),
            pltpu.VMEM((WINDOW - 2,) + slab, f32),
            pltpu.VMEM((per_block, WINDOW - 2) + slab, f32),
            *field_scratch,
        ],
        compiler_params=pltpu.CompilerParams(vmem_limit_bytes=24 << 20),
        cost_estimate=pl.CostEstimate(flops=20_000_000, bytes_accessed=8 << 20, transcendentals=0),
        name="own",
    )(plan, stiffness, nonlinear, raw, raw_other, more, more_other)

    far_along = send(far, along)
    last = lax.dynamic_slice_in_dim(near, 3 - 2 * odd, 1, 1, allow_negative_indices=False)
    edge = send(last, lambda m, y, h, c: (m, y + 1, h, c))

    basis = array(3, GROUP + per_block, slabs, *slab)
    keep, give, sums = pl.pallas_call(
        partner_kernel,
        out_shape=(basis, basis, array(n_space, 8, nz)),
        in_specs=[sm] + [vm] * 11,
        out_specs=(vm,) * 3,
        scratch_shapes=[
            pltpu.VMEM((per_block, WINDOW) + padded, f32),
            pltpu.VMEM((per_block, WINDOW) + slab, modes.dtype),
            pltpu.VMEM((per_block, WINDOW - 2) + slab, f32),
            *field_scratch,
        ],
        compiler_params=pltpu.CompilerParams(vmem_limit_bytes=24 << 20),
        cost_estimate=pl.CostEstimate(flops=40_000_000, bytes_accessed=16 << 20, transcendentals=0),
        name="partner",
    )(plan, near, far, far_along, edge, lap_own, dinv, diag, faces, moments, keep_own, give_own)

    got = send(give, partner_core)
    gathered = lax.all_to_all(sums, "space", 0, 0)

    out = pl.pallas_call(
        combine_kernel,
        out_shape=array(fields, slabs, *slab),
        in_specs=[vm] * 3,
        out_specs=vm,
        compiler_params=pltpu.CompilerParams(vmem_limit_bytes=16 << 20),
        name="combine",
    )(gathered, keep, got)
    return out.reshape((per_block, PARTNERS, slabs, ny, nz))


def solution(mesh):
    return jax.shard_map(
        shards,
        mesh=mesh,
        in_specs=(
            P("mode", "space", None, None),
            P("space", None, None),
            P(),
            P(),
            P("mode", None),
        ),
        out_specs=P("mode", None, "space", None, None),
        check_vma=False,
    )
```

```python
import jax
import jax.numpy as jnp
from jax import lax
from jax.experimental import pallas as pl
from jax.experimental.pallas import tpu as pltpu
from jax.sharding import PartitionSpec as P

PARTNERS = 3
MASS = 0.5
WINDOW = 13
OWN = 4
MOMENTS = 6
GROUP = 2
PAD = 8


f32 = jnp.float32


def clear_rims(ref, lead):
    ny = ref.shape[-2] - 2 * PAD
    zero = jnp.zeros((PAD, ref.shape[-1]), f32)
    for i in range(ref.shape[-3]):
        ref[lead + (i, pl.ds(0, PAD))] = zero
        ref[lead + (i, pl.ds(PAD + ny, PAD))] = zero


def position():
    space = lax.axis_index("space")
    return space % 2, (space // 2) % 2


def clear_window(wide):
    def clear(m, carry):
        clear_rims(wide, (m,))
        return carry

    lax.fori_loop(0, wide.shape[0], clear, 0)


def place(wide, exact, ref, slot, at):
    ny = ref.shape[2]
    for m in range(ref.shape[0]):
        wide[m, at, pl.ds(PAD, ny)] = ref[m, slot].astype(f32)
    for m in range(exact.shape[0]):
        exact[m, at] = ref[m, slot]


def spots(high):
    return 5, 9 - 8 * high, 1 + 8 * high, 0


def laplace_at(ref, lead, i, r, lane):
    nz = ref.shape[-1]
    at = PAD + r
    x = ref[lead + (i, pl.ds(at, 8))]
    left = jnp.where(lane == 0, 0.0, pltpu.roll(x, 1, 1))
    right = jnp.where(lane == nz - 1, 0.0, pltpu.roll(x, nz - 1, 1))
    rows = ref[lead + (i, pl.ds(at - 1, 8))] + ref[lead + (i, pl.ds(at + 1, 8))]
    slabs = ref[lead + (i - 1, pl.ds(at, 8))] + ref[lead + (i + 1, pl.ds(at, 8))]
    return 6.0 * x - ((rows + slabs) + (left + right))


def material(wide, label_at, stiff, cubic, gain, dinv, diag, faces):
    ny, nz = gain.shape[-2:]
    row = lax.broadcasted_iota(jnp.int32, (ny, nz), 0)
    lane = lax.broadcasted_iota(jnp.int32, (ny, nz), 1)
    body = pl.ds(PAD, ny)
    for i in range(1, 12):
        label = wide[label_at, i, body]
        c = jnp.zeros((ny, nz), f32)
        g = jnp.zeros((ny, nz), f32)
        for r in range(stiff.shape[0]):
            hit = label == float(r + 1)
            c = jnp.where(hit, stiff[r], c)
            g = jnp.where(hit, cubic[r], g)
        wide[label_at, i, body] = c
        gain[i - 1] = g
    for i in range(2, 11):
        c = wide[label_at, i, body]
        beside = (
            wide[label_at, i - 1, body],
            wide[label_at, i + 1, body],
            wide[label_at, i, pl.ds(PAD - 1, ny)],
            wide[label_at, i, pl.ds(PAD + 1, ny)],
            jnp.where(lane == 0, 0.0, pltpu.roll(c, 1, 1)),
            jnp.where(lane == nz - 1, 0.0, pltpu.roll(c, nz - 1, 1)),
        )
        ws = [0.5 * (c + n) for n in beside]
        d = MASS + ws[0] + ws[1] + ws[2] + ws[3] + ws[4] + ws[5]
        inv = jnp.where(gain[i - 1] > 0.0, 1.0 / d, 0.0)
        dinv[i - 2] = inv
        if 5 <= i < 5 + OWN:
            diag[i - 5] = d
        if 3 <= i <= 9:
            for k in range(4):
                faces[k, i - 3] = ws[k] * inv
            faces[4, i - 3] = jnp.where(lane > 0, ws[4] * inv, 0.0)
            faces[5, i - 3] = jnp.where(lane < nz - 1, ws[5] * inv, 0.0)


def krylov(group, lap_own, lap_of, j_of, shared, outs, scratch, total):
    dinv, diag, faces = shared
    keep, give = outs
    prod, v0, v1, v2 = scratch
    ny, nz = diag.shape[-2:]
    lane = lax.broadcasted_iota(jnp.int32, (8, nz), 1)
    mrow = lax.broadcasted_iota(jnp.int32, (8, nz), 0)
    rows = range(0, ny, 8)

    for t, (a, _, _) in enumerate(group):
        for i in range(1, 12):
            for r in rows:
                at = pl.ds(r, 8)
                prod[t, i, pl.ds(PAD + r, 8)] = lap_own[a, i - 1, at] * lap_of[j_of[t], i - 1, at]
    for i in range(2, 11):
        for r in rows:
            scale = -dinv[i - 2, pl.ds(r, 8)]
            for t in range(len(group)):
                v0[t, i, pl.ds(PAD + r, 8)] = laplace_at(prod, (t,), i, r, lane) * scale

    def image(ref, t, i, r, w):
        at = PAD + r
        x = ref[t, i, pl.ds(at, 8)]
        out = w[2] * ref[t, i, pl.ds(at - 1, 8)] + w[3] * ref[t, i, pl.ds(at + 1, 8)]
        out = out + (w[4] * pltpu.roll(x, 1, 1) + w[5] * pltpu.roll(x, nz - 1, 1))
        return out + (w[0] * ref[t, i - 1, pl.ds(at, 8)] + w[1] * ref[t, i + 1, pl.ds(at, 8)])

    def lower(ref, t, i, r, w):
        at = PAD + r
        x = ref[t, i, pl.ds(at, 8)]
        out = w[0] * ref[t, i - 1, pl.ds(at, 8)] + w[1] * ref[t, i, pl.ds(at - 1, 8)]
        return 2.0 * (out + w[2] * pltpu.roll(x, 1, 1)), x

    for src, dst, low, top in ((v0, v1, 3, 10), (v1, v2, 4, 9)):
        for i in range(low, top):
            for r in rows:
                w = [faces[k, i - 3, pl.ds(r, 8)] for k in range(6)]
                for t in range(len(group)):
                    dst[t, i, pl.ds(PAD + r, 8)] = image(src, t, i, r, w)

    parts = [[jnp.zeros((8, nz), f32)] * MOMENTS for _ in group]
    core, _ = position()
    for n in range(OWN):
        half, slab = n // 2, n % 2
        out = keep if half == 0 else give
        i = 5 + 2 * (core if half == 0 else 1 - core) + slab
        for r in rows:
            w = [faces[k, i - 3, pl.ds(r, 8)] for k in (0, 2, 4)]
            d = diag[i - 5, pl.ds(r, 8)]
            for t, (_, f, _) in enumerate(group):
                ring, x2 = lower(v2, t, i, r, w)
                x0, x1 = v0[t, i, pl.ds(PAD + r, 8)], v1[t, i, pl.ds(PAD + r, 8)]
                out[0, f, slab, pl.ds(r, 8)] = x0
                out[1, f, slab, pl.ds(r, 8)] = x1
                out[2, f, slab, pl.ds(r, 8)] = x2
                d0, d1, d2 = d * x0, d * x1, d * x2
                pairs = (d0 * x0, d1 * x0, d1 * x1, d2 * x1, d2 * x2, d2 * ring)
                parts[t] = [p + q for p, q in zip(parts[t], pairs)]
    for t, (_, _, column) in enumerate(group):
        col = jnp.zeros((8, nz), f32)
        for k in range(MOMENTS):
            col = jnp.where(mrow == k, jnp.sum(parts[t][k], axis=0, keepdims=True), col)
        total = jnp.where(lane == column, jnp.sum(col, axis=1, keepdims=True), total)
    return total


def laps(wide, exact, lap):
    count, places, ny, nz = lap.shape
    r = lax.broadcasted_iota(jnp.int32, (nz, nz), 0)
    c = lax.broadcasted_iota(jnp.int32, (nz, nz), 1)
    beside = jnp.where(jnp.abs(r - c) == 1, -1.0, 0.0)
    line = jnp.where(r == c, 6.0, beside).astype(exact.dtype)

    def one(m, carry):
        rows = exact[m, pl.ds(1, places)].reshape(places * ny, nz)
        lap[m] = jnp.dot(rows, line, preferred_element_type=f32).reshape(places, ny, nz)
        for i in range(1, places + 1):
            for r in range(0, ny, 8):
                at = PAD + r
                beside = wide[m, i, pl.ds(at - 1, 8)] + wide[m, i, pl.ds(at + 1, 8)]
                slabs = wide[m, i - 1, pl.ds(at, 8)] + wide[m, i + 1, pl.ds(at, 8)]
                lap[m, i - 1, pl.ds(r, 8)] = lap[m, i - 1, pl.ds(r, 8)] - (beside + slabs)
        return carry

    lax.fori_loop(0, count, one, 0)


def clear_fields(scratch):
    for ref in scratch:
        for t in range(ref.shape[0]):
            clear_rims(ref, (t,))


def pack_kernel(modes, regions, raw, ids, sems):
    blocks = modes.shape[0]
    copies = (
        pltpu.make_async_copy(regions, ids, sems.at[0]),
        pltpu.make_async_copy(modes, raw.at[pl.ds(0, blocks)], sems.at[1]),
    )
    for copy in copies:
        copy.start()
    copies[0].wait()
    raw[blocks] = (ids[...] + 1).astype(raw.dtype)
    copies[1].wait()


def own_kernel(plan, stiff, cubic, mine, other, more, more_other,
               keep, give, lap_own, dinv, diag, faces, moments,
               wide, exact, gain, lap, prod, v0, v1, v2):
    blocks, nz = lap.shape[0], lap.shape[-1]
    core, high = position()
    scratch = (prod, v0, v1, v2)
    clear_fields(scratch)
    clear_window(wide)
    here, there, beyond, edge = spots(high)
    for ref, rest, q in ((mine, more, core), (other, more_other, 1 - core)):
        for i in range(2):
            place(wide, exact, ref, i, here + 2 * q + i)
            place(wide, exact, rest, i, there + 2 * q + i)
            place(wide, exact, rest, 2 + i, beyond + 2 * q + i)

        @pl.when(q == 0)
        def _():
            place(wide, exact, rest, 4, edge)

    material(wide, blocks, stiff, cubic, gain, dinv, diag, faces)
    laps(wide, exact, lap)

    def scaled(m, carry):
        for i in range(gain.shape[0]):
            lap_own[m, i] = gain[i] * lap[m, i]
        return carry

    lax.fori_loop(0, blocks, scaled, 0)
    group = [(GROUP * core + t, t, (GROUP * core + t) * PARTNERS) for t in range(GROUP)]
    j_of = [plan[g[0], 0] for g in group]
    moments[...] = krylov(
        group, lap_own, lap, j_of, (dinv, diag, faces), (keep, give), scratch, jnp.zeros((8, nz), f32)
    )


def partner_kernel(plan, near, far, along, edge, lap_own, dinv, diag, faces, moments, keep_own, give_own,
                   keep, give, sums,
                   wide, exact, lap, prod, v0, v1, v2):
    blocks = near.shape[0]
    core, high = position()
    scratch = (prod, v0, v1, v2)
    clear_fields(scratch)
    clear_window(wide)
    for ref, first in zip((near, far, along), spots(high)):
        for k in range(OWN):
            place(wide, exact, ref, k, first + (2 * core + k if k < 2 else 2 * (1 - core) + k - 2))
    place(wide, exact, edge, 0, 0)
    for k in range(3):
        keep[k, pl.ds(0, GROUP)] = keep_own[k]
        give[k, pl.ds(0, GROUP)] = give_own[k]
    laps(wide, exact, lap)
    s = 1 + core

    def step(h, total):
        b = h * GROUP
        group = [(b + t, GROUP + b + t, (b + t) * PARTNERS + s) for t in range(GROUP)]
        j_of = [plan[g[0], s] for g in group]
        return krylov(group, lap_own, lap, j_of, (dinv, diag, faces), (keep, give), scratch, total)

    total = lax.fori_loop(0, blocks // GROUP, step, moments[...])
    for d in range(sums.shape[0]):
        sums[d] = total


def combine_kernel(sums, keep, got, out):
    m = jnp.sum(sums[...], axis=0)
    mu = [m[k : k + 1] for k in range(MOMENTS)]
    ka = [mu[k] - mu[k + 1] for k in range(MOMENTS - 1)]

    def square(c, form):
        total = None
        for i in range(len(c)):
            for j in range(i, len(c)):
                term = c[i] * c[j] * form[i + j]
                if i != j:
                    term = 2.0 * term
                total = term if total is None else total + term
        return total

    alpha = mu[0] / ka[0]
    x = [alpha, None, None]
    z = [1.0 - alpha, alpha]
    rz = square(z, mu)
    beta = rz / mu[0]
    p = [z[0] + beta, z[1]]
    alpha = rz / square(p, ka)
    x = [x[0] + alpha * p[0], alpha * p[1]]
    z = [z[0] - alpha * p[0], z[1] - alpha * (p[1] - p[0]), alpha * p[1]]
    new = square(z, mu)
    beta = new / rz
    p = [z[0] + beta * p[0], z[1] + beta * p[1], z[2]]
    alpha = new / square(p, ka)
    x = [x[0] + alpha * p[0], x[1] + alpha * p[1], alpha * p[2]]

    lane = lax.broadcasted_iota(jnp.int32, x[0].shape, 1)

    def pick(c, f):
        return jnp.sum(jnp.where(lane == f, c, 0.0), axis=1, keepdims=True)

    core, _ = position()
    for basis, q in ((keep, core), (got, 1 - core)):
        for n in range(basis.shape[1]):
            f = (GROUP * q + n) * PARTNERS if n < GROUP else (n - GROUP) * PARTNERS + 1 + q
            c0, c1, c2 = (pick(c, f) for c in x)
            for i in range(out.shape[1]):
                out[f, i] = c0 * basis[0, n, i] + c1 * basis[1, n, i] + c2 * basis[2, n, i]


def shards(modes, regions, stiffness, nonlinear, plan):
    per_block, slabs, ny, nz = modes.shape
    fields = per_block * PARTNERS
    n_mode, n_space = lax.axis_size("mode"), lax.axis_size("space")

    def send(x, to):
        pairs = []
        for m in range(n_mode):
            for s in range(n_space):
                t = to(m, s // 4, (s // 2) % 2, s % 2)
                if t is not None and 0 <= t[1] < n_space // 4:
                    tm, ty, th, tc = t
                    pairs.append((m * n_space + s, (tm % n_mode) * n_space + (ty * 2 + th) * 2 + tc))
        return lax.ppermute(x, ("mode", "space"), pairs)

    def along(m, y, h, c):
        return m, y + 1 if h == 0 else y - 1, h, c

    def partner_core(m, y, h, c):
        return m, y, h, 1 - c

    vm = pl.BlockSpec(memory_space=pltpu.VMEM)
    sm = pl.BlockSpec(memory_space=pltpu.SMEM)
    slab, padded = (ny, nz), (ny + 2 * PAD, nz)

    def array(*shape):
        return jax.ShapeDtypeStruct(shape, f32)

    raw = pl.pallas_call(
        pack_kernel,
        out_shape=jax.ShapeDtypeStruct((per_block + 1, slabs, *slab), modes.dtype),
        in_specs=[pl.BlockSpec(memory_space=pltpu.HBM)] * 2,
        out_specs=vm,
        scratch_shapes=[pltpu.VMEM((slabs,) + slab, jnp.int32), pltpu.SemaphoreType.DMA((2,))],
        compiler_params=pltpu.CompilerParams(vmem_limit_bytes=4 << 20),
        name="pack",
    )(*(pltpu.with_memory_space_constraint(v, pltpu.HBM) for v in (modes, regions)))

    odd = lax.axis_index("space") & 1
    raw_other = send(raw, partner_core)
    far0 = send(raw, lambda m, y, h, c: (m, y, 1 - h, c))
    four = jnp.concatenate([raw[:per_block], raw_other[:per_block]], 1)
    far = send(four, lambda m, y, h, c: (m + 1 + c, y, 1 - h, c))
    near = send(four, lambda m, y, h, c: (m + 1 + c, y, h, c))
    edge0 = send(raw[:, 1:], lambda m, y, h, c: (m, y + 1, h, 0) if c == 1 else None)
    far0_along = send(far0, along)
    more = jnp.concatenate([far0, far0_along, edge0], 1)
    more_other = send(more, partner_core)

    field_scratch = [pltpu.VMEM((GROUP, WINDOW) + padded, f32) for _ in range(4)]
    basis = array(3, GROUP, slabs, *slab)
    keep_own, give_own, lap_own, dinv, diag, faces, moments = pl.pallas_call(
        own_kernel,
        out_shape=(
            basis,
            basis,
            array(per_block, WINDOW - 2, *slab),
            array(WINDOW - 4, *slab),
            array(OWN, *slab),
            array(6, WINDOW - 6, *slab),
            array(8, nz),
        ),
        in_specs=[sm] * 3 + [vm] * 4,
        out_specs=(vm,) * 7,
        scratch_shapes=[
            pltpu.VMEM((per_block + 1, WINDOW) + padded, f32),
            pltpu.VMEM((per_block, WINDOW) + slab, modes.dtype),
            pltpu.VMEM((WINDOW - 2,) + slab, f32),
            pltpu.VMEM((per_block, WINDOW - 2) + slab, f32),
            *field_scratch,
        ],
        compiler_params=pltpu.CompilerParams(vmem_limit_bytes=24 << 20),
        cost_estimate=pl.CostEstimate(flops=20_000_000, bytes_accessed=8 << 20, transcendentals=0),
        name="own",
    )(plan, stiffness, nonlinear, raw, raw_other, more, more_other)

    far_along = send(far, along)
    last = lax.dynamic_slice_in_dim(near, 3 - 2 * odd, 1, 1, allow_negative_indices=False)
    edge = send(last, lambda m, y, h, c: (m, y + 1, h, c))

    basis = array(3, GROUP + per_block, slabs, *slab)
    keep, give, sums = pl.pallas_call(
        partner_kernel,
        out_shape=(basis, basis, array(n_space, 8, nz)),
        in_specs=[sm] + [vm] * 11,
        out_specs=(vm,) * 3,
        scratch_shapes=[
            pltpu.VMEM((per_block, WINDOW) + padded, f32),
            pltpu.VMEM((per_block, WINDOW) + slab, modes.dtype),
            pltpu.VMEM((per_block, WINDOW - 2) + slab, f32),
            *field_scratch,
        ],
        compiler_params=pltpu.CompilerParams(vmem_limit_bytes=24 << 20),
        cost_estimate=pl.CostEstimate(flops=40_000_000, bytes_accessed=16 << 20, transcendentals=0),
        name="partner",
    )(plan, near, far, far_along, edge, lap_own, dinv, diag, faces, moments, keep_own, give_own)

    got = send(give, partner_core)
    gathered = lax.all_to_all(sums, "space", 0, 0)

    out = pl.pallas_call(
        combine_kernel,
        out_shape=array(fields, slabs, *slab),
        in_specs=[vm] * 3,
        out_specs=vm,
        compiler_params=pltpu.CompilerParams(vmem_limit_bytes=16 << 20),
        name="combine",
    )(gathered, keep, got)
    return out.reshape((per_block, PARTNERS, slabs, ny, nz))


def solution(mesh):
    return jax.shard_map(
        shards,
        mesh=mesh,
        in_specs=(
            P("mode", "space", None, None),
            P("space", None, None),
            P(),
            P(),
            P("mode", None),
        ),
        out_specs=P("mode", None, "space", None, None),
        check_vma=False,
    )
```

```python
import jax
import jax.numpy as jnp
from jax import lax
from jax.experimental import pallas as pl
from jax.experimental.pallas import tpu as pltpu
from jax.sharding import PartitionSpec as P

PARTNERS = 3
MASS = 0.5
WINDOW = 13
OWN = 4
MOMENTS = 6
GROUP = 2
PAD = 8


f32 = jnp.float32


def clear_rims(ref, lead):
    ny = ref.shape[-2] - 2 * PAD
    zero = jnp.zeros((PAD, ref.shape[-1]), f32)
    for i in range(ref.shape[-3]):
        ref[lead + (i, pl.ds(0, PAD))] = zero
        ref[lead + (i, pl.ds(PAD + ny, PAD))] = zero


def position():
    space = lax.axis_index("space")
    return space % 2, (space // 2) % 2


def clear_window(wide):
    def clear(m, carry):
        clear_rims(wide, (m,))
        return carry

    lax.fori_loop(0, wide.shape[0], clear, 0)


def place(wide, exact, ref, slot, at):
    ny = ref.shape[2]
    for m in range(ref.shape[0]):
        wide[m, at, pl.ds(PAD, ny)] = ref[m, slot].astype(f32)
    for m in range(exact.shape[0]):
        exact[m, at] = ref[m, slot]


def spots(high):
    return 5, 9 - 8 * high, 1 + 8 * high, 0


def laplace_at(ref, lead, i, r, lane):
    nz = ref.shape[-1]
    at = PAD + r
    x = ref[lead + (i, pl.ds(at, 8))]
    left = jnp.where(lane == 0, 0.0, pltpu.roll(x, 1, 1))
    right = jnp.where(lane == nz - 1, 0.0, pltpu.roll(x, nz - 1, 1))
    rows = ref[lead + (i, pl.ds(at - 1, 8))] + ref[lead + (i, pl.ds(at + 1, 8))]
    slabs = ref[lead + (i - 1, pl.ds(at, 8))] + ref[lead + (i + 1, pl.ds(at, 8))]
    return 6.0 * x - ((rows + slabs) + (left + right))


def material(wide, label_at, stiff, cubic, gain, dinv, diag, faces):
    ny, nz = gain.shape[-2:]
    row = lax.broadcasted_iota(jnp.int32, (ny, nz), 0)
    lane = lax.broadcasted_iota(jnp.int32, (ny, nz), 1)
    body = pl.ds(PAD, ny)
    for i in range(1, 12):
        label = wide[label_at, i, body]
        c = jnp.zeros((ny, nz), f32)
        g = jnp.zeros((ny, nz), f32)
        for r in range(stiff.shape[0]):
            hit = label == float(r + 1)
            c = jnp.where(hit, stiff[r], c)
            g = jnp.where(hit, cubic[r], g)
        wide[label_at, i, body] = c
        gain[i - 1] = g
    for i in range(2, 11):
        c = wide[label_at, i, body]
        beside = (
            wide[label_at, i - 1, body],
            wide[label_at, i + 1, body],
            wide[label_at, i, pl.ds(PAD - 1, ny)],
            wide[label_at, i, pl.ds(PAD + 1, ny)],
            jnp.where(lane == 0, 0.0, pltpu.roll(c, 1, 1)),
            jnp.where(lane == nz - 1, 0.0, pltpu.roll(c, nz - 1, 1)),
        )
        ws = [0.5 * (c + n) for n in beside]
        d = MASS + ws[0] + ws[1] + ws[2] + ws[3] + ws[4] + ws[5]
        inv = jnp.where(gain[i - 1] > 0.0, 1.0 / d, 0.0)
        dinv[i - 2] = inv
        if 5 <= i < 5 + OWN:
            diag[i - 5] = d
        if 3 <= i <= 9:
            for k in range(4):
                faces[k, i - 3] = ws[k] * inv
            faces[4, i - 3] = jnp.where(lane > 0, ws[4] * inv, 0.0)
            faces[5, i - 3] = jnp.where(lane < nz - 1, ws[5] * inv, 0.0)


def krylov(group, lap_own, lap_of, j_of, shared, outs, scratch, total):
    dinv, diag, faces = shared
    keep, give = outs
    prod, v0, v1, v2 = scratch
    ny, nz = diag.shape[-2:]
    lane = lax.broadcasted_iota(jnp.int32, (8, nz), 1)
    mrow = lax.broadcasted_iota(jnp.int32, (8, nz), 0)
    rows = range(0, ny, 8)

    for t, (a, _, _) in enumerate(group):
        for i in range(1, 12):
            for r in rows:
                at = pl.ds(r, 8)
                prod[t, i, pl.ds(PAD + r, 8)] = lap_own[a, i - 1, at] * lap_of[j_of[t], i - 1, at]
    for i in range(2, 11):
        for r in rows:
            scale = -dinv[i - 2, pl.ds(r, 8)]
            for t in range(len(group)):
                v0[t, i, pl.ds(PAD + r, 8)] = laplace_at(prod, (t,), i, r, lane) * scale

    def image(ref, t, i, r, w):
        at = PAD + r
        x = ref[t, i, pl.ds(at, 8)]
        out = w[2] * ref[t, i, pl.ds(at - 1, 8)] + w[3] * ref[t, i, pl.ds(at + 1, 8)]
        out = out + (w[4] * pltpu.roll(x, 1, 1) + w[5] * pltpu.roll(x, nz - 1, 1))
        return out + (w[0] * ref[t, i - 1, pl.ds(at, 8)] + w[1] * ref[t, i + 1, pl.ds(at, 8)])

    def lower(ref, t, i, r, w):
        at = PAD + r
        x = ref[t, i, pl.ds(at, 8)]
        out = w[0] * ref[t, i - 1, pl.ds(at, 8)] + w[1] * ref[t, i, pl.ds(at - 1, 8)]
        return 2.0 * (out + w[2] * pltpu.roll(x, 1, 1)), x

    for src, dst, low, top in ((v0, v1, 3, 10), (v1, v2, 4, 9)):
        for i in range(low, top):
            for r in rows:
                w = [faces[k, i - 3, pl.ds(r, 8)] for k in range(6)]
                for t in range(len(group)):
                    dst[t, i, pl.ds(PAD + r, 8)] = image(src, t, i, r, w)

    parts = [[jnp.zeros((8, nz), f32)] * MOMENTS for _ in group]
    core, _ = position()
    for n in range(OWN):
        half, slab = n // 2, n % 2
        out = keep if half == 0 else give
        i = 5 + 2 * (core if half == 0 else 1 - core) + slab
        for r in rows:
            w = [faces[k, i - 3, pl.ds(r, 8)] for k in (0, 2, 4)]
            d = diag[i - 5, pl.ds(r, 8)]
            for t, (_, f, _) in enumerate(group):
                ring, x2 = lower(v2, t, i, r, w)
                x0, x1 = v0[t, i, pl.ds(PAD + r, 8)], v1[t, i, pl.ds(PAD + r, 8)]
                out[0, f, slab, pl.ds(r, 8)] = x0
                out[1, f, slab, pl.ds(r, 8)] = x1
                out[2, f, slab, pl.ds(r, 8)] = x2
                d0, d1, d2 = d * x0, d * x1, d * x2
                pairs = (d0 * x0, d1 * x0, d1 * x1, d2 * x1, d2 * x2, d2 * ring)
                parts[t] = [p + q for p, q in zip(parts[t], pairs)]
    for t, (_, _, column) in enumerate(group):
        col = jnp.zeros((8, nz), f32)
        for k in range(MOMENTS):
            col = jnp.where(mrow == k, jnp.sum(parts[t][k], axis=0, keepdims=True), col)
        total = jnp.where(lane == column, jnp.sum(col, axis=1, keepdims=True), total)
    return total


def laps(wide, exact, lap):
    count, places, ny, nz = lap.shape
    r = lax.broadcasted_iota(jnp.int32, (nz, nz), 0)
    c = lax.broadcasted_iota(jnp.int32, (nz, nz), 1)
    beside = jnp.where(jnp.abs(r - c) == 1, -1.0, 0.0)
    line = jnp.where(r == c, 6.0, beside).astype(exact.dtype)

    def one(m, carry):
        rows = exact[m, pl.ds(1, places)].reshape(places * ny, nz)
        lap[m] = jnp.dot(rows, line, preferred_element_type=f32).reshape(places, ny, nz)
        for i in range(1, places + 1):
            for r in range(0, ny, 8):
                at = PAD + r
                beside = wide[m, i, pl.ds(at - 1, 8)] + wide[m, i, pl.ds(at + 1, 8)]
                slabs = wide[m, i - 1, pl.ds(at, 8)] + wide[m, i + 1, pl.ds(at, 8)]
                lap[m, i - 1, pl.ds(r, 8)] = lap[m, i - 1, pl.ds(r, 8)] - (beside + slabs)
        return carry

    lax.fori_loop(0, count, one, 0)


def clear_fields(scratch):
    for ref in scratch:
        for t in range(ref.shape[0]):
            clear_rims(ref, (t,))


def pack_kernel(modes, regions, raw, ids, sems):
    blocks = modes.shape[0]
    copies = (
        pltpu.make_async_copy(regions, ids, sems.at[0]),
        pltpu.make_async_copy(modes, raw.at[pl.ds(0, blocks)], sems.at[1]),
    )
    for copy in copies:
        copy.start()
    copies[0].wait()
    raw[blocks] = (ids[...] + 1).astype(raw.dtype)
    copies[1].wait()


def own_kernel(plan, stiff, cubic, mine, other, more, more_other,
               keep, give, lap_own, dinv, diag, faces, moments,
               wide, exact, gain, lap, prod, v0, v1, v2):
    blocks, nz = lap.shape[0], lap.shape[-1]
    core, high = position()
    scratch = (prod, v0, v1, v2)
    clear_fields(scratch)
    clear_window(wide)
    here, there, beyond, edge = spots(high)
    for ref, rest, q in ((mine, more, core), (other, more_other, 1 - core)):
        for i in range(2):
            place(wide, exact, ref, i, here + 2 * q + i)
            place(wide, exact, rest, i, there + 2 * q + i)
            place(wide, exact, rest, 2 + i, beyond + 2 * q + i)

        @pl.when(q == 0)
        def _():
            place(wide, exact, rest, 4, edge)

    material(wide, blocks, stiff, cubic, gain, dinv, diag, faces)
    laps(wide, exact, lap)

    def scaled(m, carry):
        for i in range(gain.shape[0]):
            lap_own[m, i] = gain[i] * lap[m, i]
        return carry

    lax.fori_loop(0, blocks, scaled, 0)
    group = [(GROUP * core + t, t, (GROUP * core + t) * PARTNERS) for t in range(GROUP)]
    j_of = [plan[g[0], 0] for g in group]
    moments[...] = krylov(
        group, lap_own, lap, j_of, (dinv, diag, faces), (keep, give), scratch, jnp.zeros((8, nz), f32)
    )


def partner_kernel(plan, near, far, along, edge, lap_own, dinv, diag, faces, moments, keep_own, give_own,
                   keep, give, sums,
                   wide, exact, lap, prod, v0, v1, v2):
    blocks = near.shape[0]
    core, high = position()
    scratch = (prod, v0, v1, v2)
    clear_fields(scratch)
    clear_window(wide)
    for ref, first in zip((near, far, along), spots(high)):
        for k in range(OWN):
            place(wide, exact, ref, k, first + (2 * core + k if k < 2 else 2 * (1 - core) + k - 2))
    place(wide, exact, edge, 0, 0)
    for k in range(3):
        keep[k, pl.ds(0, GROUP)] = keep_own[k]
        give[k, pl.ds(0, GROUP)] = give_own[k]
    laps(wide, exact, lap)
    s = 1 + core

    def step(h, total):
        b = h * GROUP
        group = [(b + t, GROUP + b + t, (b + t) * PARTNERS + s) for t in range(GROUP)]
        j_of = [plan[g[0], s] for g in group]
        return krylov(group, lap_own, lap, j_of, (dinv, diag, faces), (keep, give), scratch, total)

    total = lax.fori_loop(0, blocks // GROUP, step, moments[...])
    for d in range(sums.shape[0]):
        sums[d] = total


def combine_kernel(sums, keep, got, out, held, sems):
    m = jnp.sum(sums[...], axis=0)
    mu = [m[k : k + 1] for k in range(MOMENTS)]
    ka = [mu[k] - mu[k + 1] for k in range(MOMENTS - 1)]

    def square(c, form):
        total = None
        for i in range(len(c)):
            for j in range(i, len(c)):
                term = c[i] * c[j] * form[i + j]
                if i != j:
                    term = 2.0 * term
                total = term if total is None else total + term
        return total

    alpha = mu[0] / ka[0]
    x = [alpha, None, None]
    z = [1.0 - alpha, alpha]
    rz = square(z, mu)
    beta = rz / mu[0]
    p = [z[0] + beta, z[1]]
    alpha = rz / square(p, ka)
    x = [x[0] + alpha * p[0], alpha * p[1]]
    z = [z[0] - alpha * p[0], z[1] - alpha * (p[1] - p[0]), alpha * p[1]]
    new = square(z, mu)
    beta = new / rz
    p = [z[0] + beta * p[0], z[1] + beta * p[1], z[2]]
    alpha = new / square(p, ka)
    x = [x[0] + alpha * p[0], x[1] + alpha * p[1], alpha * p[2]]

    lane = lax.broadcasted_iota(jnp.int32, x[0].shape, 1)

    def pick(c, f):
        return jnp.sum(jnp.where(lane == f, c, 0.0), axis=1, keepdims=True)

    core, _ = position()
    copies = []
    for basis, q in ((keep, core), (got, 1 - core)):
        for n in range(basis.shape[1]):
            f = (GROUP * q + n) * PARTNERS if n < GROUP else (n - GROUP) * PARTNERS + 1 + q
            c0, c1, c2 = (pick(c, f) for c in x)
            at = n if basis is keep else basis.shape[1] + n
            for i in range(out.shape[1]):
                held[at, i] = c0 * basis[0, n, i] + c1 * basis[1, n, i] + c2 * basis[2, n, i]
            copies.append(pltpu.make_async_copy(held.at[at], out.at[f], sems.at[at]))
            copies[-1].start()
    for copy in copies:
        copy.wait()


def shards(modes, regions, stiffness, nonlinear, plan):
    per_block, slabs, ny, nz = modes.shape
    fields = per_block * PARTNERS
    n_mode, n_space = lax.axis_size("mode"), lax.axis_size("space")

    def send(x, to):
        pairs = []
        for m in range(n_mode):
            for s in range(n_space):
                t = to(m, s // 4, (s // 2) % 2, s % 2)
                if t is not None and 0 <= t[1] < n_space // 4:
                    tm, ty, th, tc = t
                    pairs.append((m * n_space + s, (tm % n_mode) * n_space + (ty * 2 + th) * 2 + tc))
        return lax.ppermute(x, ("mode", "space"), pairs)

    def along(m, y, h, c):
        return m, y + 1 if h == 0 else y - 1, h, c

    def partner_core(m, y, h, c):
        return m, y, h, 1 - c

    vm = pl.BlockSpec(memory_space=pltpu.VMEM)
    sm = pl.BlockSpec(memory_space=pltpu.SMEM)
    slab, padded = (ny, nz), (ny + 2 * PAD, nz)

    def array(*shape):
        return jax.ShapeDtypeStruct(shape, f32)

    raw = pl.pallas_call(
        pack_kernel,
        out_shape=jax.ShapeDtypeStruct((per_block + 1, slabs, *slab), modes.dtype),
        in_specs=[pl.BlockSpec(memory_space=pltpu.HBM)] * 2,
        out_specs=vm,
        scratch_shapes=[pltpu.VMEM((slabs,) + slab, jnp.int32), pltpu.SemaphoreType.DMA((2,))],
        compiler_params=pltpu.CompilerParams(vmem_limit_bytes=4 << 20),
        name="pack",
    )(*(pltpu.with_memory_space_constraint(v, pltpu.HBM) for v in (modes, regions)))

    odd = lax.axis_index("space") & 1
    raw_other = send(raw, partner_core)
    far0 = send(raw, lambda m, y, h, c: (m, y, 1 - h, c))
    four = jnp.concatenate([raw[:per_block], raw_other[:per_block]], 1)
    far = send(four, lambda m, y, h, c: (m + 1 + c, y, 1 - h, c))
    near = send(four, lambda m, y, h, c: (m + 1 + c, y, h, c))
    edge0 = send(raw[:, 1:], lambda m, y, h, c: (m, y + 1, h, 0) if c == 1 else None)
    far0_along = send(far0, along)
    more = jnp.concatenate([far0, far0_along, edge0], 1)
    more_other = send(more, partner_core)

    field_scratch = [pltpu.VMEM((GROUP, WINDOW) + padded, f32) for _ in range(4)]
    basis = array(3, GROUP, slabs, *slab)
    keep_own, give_own, lap_own, dinv, diag, faces, moments = pl.pallas_call(
        own_kernel,
        out_shape=(
            basis,
            basis,
            array(per_block, WINDOW - 2, *slab),
            array(WINDOW - 4, *slab),
            array(OWN, *slab),
            array(6, WINDOW - 6, *slab),
            array(8, nz),
        ),
        in_specs=[sm] * 3 + [vm] * 4,
        out_specs=(vm,) * 7,
        scratch_shapes=[
            pltpu.VMEM((per_block + 1, WINDOW) + padded, f32),
            pltpu.VMEM((per_block, WINDOW) + slab, modes.dtype),
            pltpu.VMEM((WINDOW - 2,) + slab, f32),
            pltpu.VMEM((per_block, WINDOW - 2) + slab, f32),
            *field_scratch,
        ],
        compiler_params=pltpu.CompilerParams(vmem_limit_bytes=24 << 20),
        cost_estimate=pl.CostEstimate(flops=20_000_000, bytes_accessed=8 << 20, transcendentals=0),
        name="own",
    )(plan, stiffness, nonlinear, raw, raw_other, more, more_other)

    far_along = send(far, along)
    last = lax.dynamic_slice_in_dim(near, 3 - 2 * odd, 1, 1, allow_negative_indices=False)
    edge = send(last, lambda m, y, h, c: (m, y + 1, h, c))

    basis = array(3, GROUP + per_block, slabs, *slab)
    keep, give, sums = pl.pallas_call(
        partner_kernel,
        out_shape=(basis, basis, array(n_space, 8, nz)),
        in_specs=[sm] + [vm] * 11,
        out_specs=(vm,) * 3,
        scratch_shapes=[
            pltpu.VMEM((per_block, WINDOW) + padded, f32),
            pltpu.VMEM((per_block, WINDOW) + slab, modes.dtype),
            pltpu.VMEM((per_block, WINDOW - 2) + slab, f32),
            *field_scratch,
        ],
        compiler_params=pltpu.CompilerParams(vmem_limit_bytes=24 << 20),
        cost_estimate=pl.CostEstimate(flops=40_000_000, bytes_accessed=16 << 20, transcendentals=0),
        name="partner",
    )(plan, near, far, far_along, edge, lap_own, dinv, diag, faces, moments, keep_own, give_own)

    got = send(give, partner_core)
    gathered = lax.all_to_all(sums, "space", 0, 0)

    out = pl.pallas_call(
        combine_kernel,
        out_shape=array(fields, slabs, *slab),
        in_specs=[vm] * 3,
        out_specs=pl.BlockSpec(memory_space=pltpu.HBM),
        scratch_shapes=[pltpu.VMEM((fields, slabs) + slab, f32), pltpu.SemaphoreType.DMA((fields,))],
        compiler_params=pltpu.CompilerParams(vmem_limit_bytes=16 << 20),
        name="combine",
    )(gathered, keep, got)
    return out.reshape((per_block, PARTNERS, slabs, ny, nz))


def solution(mesh):
    return jax.shard_map(
        shards,
        mesh=mesh,
        in_specs=(
            P("mode", "space", None, None),
            P("space", None, None),
            P(),
            P(),
            P("mode", None),
        ),
        out_specs=P("mode", None, "space", None, None),
        check_vma=False,
    )
```

```python
import jax
import jax.numpy as jnp
from jax import lax
from jax.experimental import pallas as pl
from jax.experimental.pallas import tpu as pltpu
from jax.sharding import PartitionSpec as P

PARTNERS = 3
MASS = 0.5
WINDOW = 13
OWN = 4
MOMENTS = 6
GROUP = 2
PAD = 8


f32 = jnp.float32


def clear_rims(ref, lead):
    ny = ref.shape[-2] - 2 * PAD
    zero = jnp.zeros((PAD, ref.shape[-1]), f32)
    for i in range(ref.shape[-3]):
        ref[lead + (i, pl.ds(0, PAD))] = zero
        ref[lead + (i, pl.ds(PAD + ny, PAD))] = zero


def position():
    space = lax.axis_index("space")
    return space % 2, (space // 2) % 2


def clear_window(wide):
    def clear(m, carry):
        clear_rims(wide, (m,))
        return carry

    lax.fori_loop(0, wide.shape[0], clear, 0)


def place(wide, exact, ref, slot, at):
    ny = ref.shape[2]
    for m in range(ref.shape[0]):
        wide[m, at, pl.ds(PAD, ny)] = ref[m, slot].astype(f32)
    for m in range(exact.shape[0]):
        exact[m, at] = ref[m, slot]


def spots(high):
    return 5, 9 - 8 * high, 1 + 8 * high, 0


def laplace_at(ref, lead, i, r, lane):
    nz = ref.shape[-1]
    at = PAD + r
    x = ref[lead + (i, pl.ds(at, 8))]
    left = jnp.where(lane == 0, 0.0, pltpu.roll(x, 1, 1))
    right = jnp.where(lane == nz - 1, 0.0, pltpu.roll(x, nz - 1, 1))
    rows = ref[lead + (i, pl.ds(at - 1, 8))] + ref[lead + (i, pl.ds(at + 1, 8))]
    slabs = ref[lead + (i - 1, pl.ds(at, 8))] + ref[lead + (i + 1, pl.ds(at, 8))]
    return 6.0 * x - ((rows + slabs) + (left + right))


def material(wide, label_at, stiff, cubic, gain, dinv, diag, faces):
    ny, nz = gain.shape[-2:]
    row = lax.broadcasted_iota(jnp.int32, (ny, nz), 0)
    lane = lax.broadcasted_iota(jnp.int32, (ny, nz), 1)
    body = pl.ds(PAD, ny)
    for i in range(1, 12):
        label = wide[label_at, i, body]
        c = jnp.zeros((ny, nz), f32)
        g = jnp.zeros((ny, nz), f32)
        for r in range(stiff.shape[0]):
            hit = label == float(r + 1)
            c = jnp.where(hit, stiff[r], c)
            g = jnp.where(hit, cubic[r], g)
        wide[label_at, i, body] = c
        gain[i - 1] = g
    for i in range(2, 11):
        c = wide[label_at, i, body]
        beside = (
            wide[label_at, i - 1, body],
            wide[label_at, i + 1, body],
            wide[label_at, i, pl.ds(PAD - 1, ny)],
            wide[label_at, i, pl.ds(PAD + 1, ny)],
            jnp.where(lane == 0, 0.0, pltpu.roll(c, 1, 1)),
            jnp.where(lane == nz - 1, 0.0, pltpu.roll(c, nz - 1, 1)),
        )
        ws = [0.5 * (c + n) for n in beside]
        d = MASS + ws[0] + ws[1] + ws[2] + ws[3] + ws[4] + ws[5]
        inv = jnp.where(gain[i - 1] > 0.0, 1.0 / d, 0.0)
        dinv[i - 2] = inv
        if 5 <= i < 5 + OWN:
            diag[i - 5] = d
        if 3 <= i <= 9:
            for k in range(4):
                faces[k, i - 3] = ws[k] * inv
            faces[4, i - 3] = jnp.where(lane > 0, ws[4] * inv, 0.0)
            faces[5, i - 3] = jnp.where(lane < nz - 1, ws[5] * inv, 0.0)


def krylov(group, lap_own, lap_of, j_of, shared, outs, scratch, total):
    dinv, diag, faces = shared
    keep, give = outs
    prod, v0, v1, v2 = scratch
    ny, nz = diag.shape[-2:]
    lane = lax.broadcasted_iota(jnp.int32, (8, nz), 1)
    mrow = lax.broadcasted_iota(jnp.int32, (8, nz), 0)
    rows = range(0, ny, 8)

    for t, (a, _, _) in enumerate(group):
        for i in range(1, 12):
            for r in rows:
                at = pl.ds(r, 8)
                prod[t, i, pl.ds(PAD + r, 8)] = lap_own[a, i - 1, at] * lap_of[j_of[t], i - 1, at]
    for i in range(2, 11):
        for r in rows:
            scale = -dinv[i - 2, pl.ds(r, 8)]
            for t in range(len(group)):
                v0[t, i, pl.ds(PAD + r, 8)] = laplace_at(prod, (t,), i, r, lane) * scale

    def image(ref, t, i, r, w):
        at = PAD + r
        x = ref[t, i, pl.ds(at, 8)]
        out = w[2] * ref[t, i, pl.ds(at - 1, 8)] + w[3] * ref[t, i, pl.ds(at + 1, 8)]
        out = out + (w[4] * pltpu.roll(x, 1, 1) + w[5] * pltpu.roll(x, nz - 1, 1))
        return out + (w[0] * ref[t, i - 1, pl.ds(at, 8)] + w[1] * ref[t, i + 1, pl.ds(at, 8)])

    def lower(ref, t, i, r, w):
        at = PAD + r
        x = ref[t, i, pl.ds(at, 8)]
        out = w[0] * ref[t, i - 1, pl.ds(at, 8)] + w[1] * ref[t, i, pl.ds(at - 1, 8)]
        return 2.0 * (out + w[2] * pltpu.roll(x, 1, 1)), x

    for src, dst, low, top in ((v0, v1, 3, 10), (v1, v2, 4, 9)):
        for i in range(low, top):
            for r in rows:
                w = [faces[k, i - 3, pl.ds(r, 8)] for k in range(6)]
                for t in range(len(group)):
                    dst[t, i, pl.ds(PAD + r, 8)] = image(src, t, i, r, w)

    parts = [[jnp.zeros((8, nz), f32)] * MOMENTS for _ in group]
    core, _ = position()
    for n in range(OWN):
        half, slab = n // 2, n % 2
        out = keep if half == 0 else give
        i = 5 + 2 * (core if half == 0 else 1 - core) + slab
        for r in rows:
            w = [faces[k, i - 3, pl.ds(r, 8)] for k in (0, 2, 4)]
            d = diag[i - 5, pl.ds(r, 8)]
            for t, (_, f, _) in enumerate(group):
                ring, x2 = lower(v2, t, i, r, w)
                x0, x1 = v0[t, i, pl.ds(PAD + r, 8)], v1[t, i, pl.ds(PAD + r, 8)]
                out[0, f, slab, pl.ds(r, 8)] = x0
                out[1, f, slab, pl.ds(r, 8)] = x1
                out[2, f, slab, pl.ds(r, 8)] = x2
                d0, d1, d2 = d * x0, d * x1, d * x2
                pairs = (d0 * x0, d1 * x0, d1 * x1, d2 * x1, d2 * x2, d2 * ring)
                parts[t] = [p + q for p, q in zip(parts[t], pairs)]
    for t, (_, _, column) in enumerate(group):
        col = jnp.zeros((8, nz), f32)
        for k in range(MOMENTS):
            col = jnp.where(mrow == k, jnp.sum(parts[t][k], axis=0, keepdims=True), col)
        total = jnp.where(lane == column, jnp.sum(col, axis=1, keepdims=True), total)
    return total


def laps(wide, exact, lap):
    count, places, ny, nz = lap.shape
    r = lax.broadcasted_iota(jnp.int32, (nz, nz), 0)
    c = lax.broadcasted_iota(jnp.int32, (nz, nz), 1)
    beside = jnp.where(jnp.abs(r - c) == 1, -1.0, 0.0)
    line = jnp.where(r == c, 6.0, beside).astype(exact.dtype)

    def one(m, carry):
        rows = exact[m, pl.ds(1, places)].reshape(places * ny, nz)
        lap[m] = jnp.dot(rows, line, preferred_element_type=f32).reshape(places, ny, nz)
        for i in range(1, places + 1):
            for r in range(0, ny, 8):
                at = PAD + r
                beside = wide[m, i, pl.ds(at - 1, 8)] + wide[m, i, pl.ds(at + 1, 8)]
                slabs = wide[m, i - 1, pl.ds(at, 8)] + wide[m, i + 1, pl.ds(at, 8)]
                lap[m, i - 1, pl.ds(r, 8)] = lap[m, i - 1, pl.ds(r, 8)] - (beside + slabs)
        return carry

    lax.fori_loop(0, count, one, 0)


def clear_fields(scratch):
    for ref in scratch:
        for t in range(ref.shape[0]):
            clear_rims(ref, (t,))


def pack_kernel(modes, regions, raw, ids, sems):
    blocks = modes.shape[0]
    copies = (
        pltpu.make_async_copy(regions, ids, sems.at[0]),
        pltpu.make_async_copy(modes, raw.at[pl.ds(0, blocks)], sems.at[1]),
    )
    for copy in copies:
        copy.start()
    copies[0].wait()
    raw[blocks] = (ids[...] + 1).astype(raw.dtype)
    copies[1].wait()


def own_kernel(plan, stiff, cubic, mine, other, more, more_other, last,
               keep, give, lap_own, dinv, diag, faces, moments,
               wide, exact, gain, lap, prod, v0, v1, v2):
    blocks, nz = lap.shape[0], lap.shape[-1]
    core, high = position()
    scratch = (prod, v0, v1, v2)
    clear_fields(scratch)
    clear_window(wide)
    here, there, beyond, edge = spots(high)
    for ref, rest, q in ((mine, more, core), (other, more_other, 1 - core)):
        for i in range(2):
            place(wide, exact, ref, i, here + 2 * q + i)
            place(wide, exact, rest, i, there + 2 * q + i)
            place(wide, exact, rest, 2 + i, beyond + 2 * q + i)
    place(wide, exact, last, 0, edge)

    material(wide, blocks, stiff, cubic, gain, dinv, diag, faces)
    laps(wide, exact, lap)

    def scaled(m, carry):
        for i in range(gain.shape[0]):
            lap_own[m, i] = gain[i] * lap[m, i]
        return carry

    lax.fori_loop(0, blocks, scaled, 0)
    group = [(GROUP * core + t, t, (GROUP * core + t) * PARTNERS) for t in range(GROUP)]
    j_of = [plan[g[0], 0] for g in group]
    moments[...] = krylov(
        group, lap_own, lap, j_of, (dinv, diag, faces), (keep, give), scratch, jnp.zeros((8, nz), f32)
    )


def partner_kernel(plan, near, far, along, lap_own, dinv, diag, faces, moments, keep_own, give_own,
                   keep, give, sums,
                   wide, exact, lap, prod, v0, v1, v2):
    blocks = near.shape[0]
    core, high = position()
    scratch = (prod, v0, v1, v2)
    clear_fields(scratch)
    clear_window(wide)
    for ref, first in zip((near, far, along), spots(high)):
        for k in range(OWN):
            place(wide, exact, ref, k, first + (2 * core + k if k < 2 else 2 * (1 - core) + k - 2))
    place(wide, exact, near, OWN, 0)
    for k in range(3):
        keep[k, pl.ds(0, GROUP)] = keep_own[k]
        give[k, pl.ds(0, GROUP)] = give_own[k]
    laps(wide, exact, lap)
    s = 1 + core

    def step(h, total):
        b = h * GROUP
        group = [(b + t, GROUP + b + t, (b + t) * PARTNERS + s) for t in range(GROUP)]
        j_of = [plan[g[0], s] for g in group]
        return krylov(group, lap_own, lap, j_of, (dinv, diag, faces), (keep, give), scratch, total)

    total = lax.fori_loop(0, blocks // GROUP, step, moments[...])
    for d in range(sums.shape[0]):
        sums[d] = total


def combine_kernel(sums, keep, got, out, held, sems):
    m = jnp.sum(sums[...], axis=0)
    mu = [m[k : k + 1] for k in range(MOMENTS)]
    ka = [mu[k] - mu[k + 1] for k in range(MOMENTS - 1)]

    def square(c, form):
        total = None
        for i in range(len(c)):
            for j in range(i, len(c)):
                term = c[i] * c[j] * form[i + j]
                if i != j:
                    term = 2.0 * term
                total = term if total is None else total + term
        return total

    alpha = mu[0] / ka[0]
    x = [alpha, None, None]
    z = [1.0 - alpha, alpha]
    rz = square(z, mu)
    beta = rz / mu[0]
    p = [z[0] + beta, z[1]]
    alpha = rz / square(p, ka)
    x = [x[0] + alpha * p[0], alpha * p[1]]
    z = [z[0] - alpha * p[0], z[1] - alpha * (p[1] - p[0]), alpha * p[1]]
    new = square(z, mu)
    beta = new / rz
    p = [z[0] + beta * p[0], z[1] + beta * p[1], z[2]]
    alpha = new / square(p, ka)
    x = [x[0] + alpha * p[0], x[1] + alpha * p[1], alpha * p[2]]

    lane = lax.broadcasted_iota(jnp.int32, x[0].shape, 1)

    def pick(c, f):
        return jnp.sum(jnp.where(lane == f, c, 0.0), axis=1, keepdims=True)

    core, _ = position()
    copies = []
    for basis, q in ((keep, core), (got, 1 - core)):
        for n in range(basis.shape[1]):
            f = (GROUP * q + n) * PARTNERS if n < GROUP else (n - GROUP) * PARTNERS + 1 + q
            c0, c1, c2 = (pick(c, f) for c in x)
            at = n if basis is keep else basis.shape[1] + n
            for i in range(out.shape[1]):
                held[at, i] = c0 * basis[0, n, i] + c1 * basis[1, n, i] + c2 * basis[2, n, i]
            copies.append(pltpu.make_async_copy(held.at[at], out.at[f], sems.at[at]))
            copies[-1].start()
    for copy in copies:
        copy.wait()


def shards(modes, regions, stiffness, nonlinear, plan):
    per_block, slabs, ny, nz = modes.shape
    fields = per_block * PARTNERS
    n_mode, n_space = lax.axis_size("mode"), lax.axis_size("space")

    def send(x, to):
        pairs = []
        for m in range(n_mode):
            for s in range(n_space):
                t = to(m, s // 4, (s // 2) % 2, s % 2)
                if t is not None and 0 <= t[1] < n_space // 4:
                    tm, ty, th, tc = t
                    pairs.append((m * n_space + s, (tm % n_mode) * n_space + (ty * 2 + th) * 2 + tc))
        return lax.ppermute(x, ("mode", "space"), pairs)

    def along(m, y, h, c):
        return m, y + 1 if h == 0 else y - 1, h, c

    def partner_core(m, y, h, c):
        return m, y, h, 1 - c

    vm = pl.BlockSpec(memory_space=pltpu.VMEM)
    sm = pl.BlockSpec(memory_space=pltpu.SMEM)
    slab, padded = (ny, nz), (ny + 2 * PAD, nz)

    def array(*shape):
        return jax.ShapeDtypeStruct(shape, f32)

    raw = pl.pallas_call(
        pack_kernel,
        out_shape=jax.ShapeDtypeStruct((per_block + 1, slabs, *slab), modes.dtype),
        in_specs=[pl.BlockSpec(memory_space=pltpu.HBM)] * 2,
        out_specs=vm,
        scratch_shapes=[pltpu.VMEM((slabs,) + slab, jnp.int32), pltpu.SemaphoreType.DMA((2,))],
        compiler_params=pltpu.CompilerParams(vmem_limit_bytes=4 << 20),
        name="pack",
    )(*(pltpu.with_memory_space_constraint(v, pltpu.HBM) for v in (modes, regions)))

    odd = lax.axis_index("space") & 1
    raw_other = send(raw, partner_core)
    far0 = send(raw, lambda m, y, h, c: (m, y, 1 - h, c))
    chip = jnp.concatenate([raw, raw_other], 1)
    four = chip[:per_block]
    last = lax.dynamic_slice_in_dim(chip, 3 - 2 * odd, 1, 1, allow_negative_indices=False)
    edge = send(last, lambda m, y, h, c: (m, y + 1, h, c))
    far = send(four, lambda m, y, h, c: (m + 1 + c, y, 1 - h, c))
    five = jnp.concatenate([four, edge[:per_block]], 1)
    near = send(five, lambda m, y, h, c: (m + 1 + c, y, h, c))
    far0_along = send(far0, along)
    more = jnp.concatenate([far0, far0_along], 1)
    more_other = send(more, partner_core)

    field_scratch = [pltpu.VMEM((GROUP, WINDOW) + padded, f32) for _ in range(4)]
    basis = array(3, GROUP, slabs, *slab)
    keep_own, give_own, lap_own, dinv, diag, faces, moments = pl.pallas_call(
        own_kernel,
        out_shape=(
            basis,
            basis,
            array(per_block, WINDOW - 2, *slab),
            array(WINDOW - 4, *slab),
            array(OWN, *slab),
            array(6, WINDOW - 6, *slab),
            array(8, nz),
        ),
        in_specs=[sm] * 3 + [vm] * 5,
        out_specs=(vm,) * 7,
        scratch_shapes=[
            pltpu.VMEM((per_block + 1, WINDOW) + padded, f32),
            pltpu.VMEM((per_block, WINDOW) + slab, modes.dtype),
            pltpu.VMEM((WINDOW - 2,) + slab, f32),
            pltpu.VMEM((per_block, WINDOW - 2) + slab, f32),
            *field_scratch,
        ],
        compiler_params=pltpu.CompilerParams(vmem_limit_bytes=24 << 20),
        cost_estimate=pl.CostEstimate(flops=20_000_000, bytes_accessed=8 << 20, transcendentals=0),
        name="own",
    )(plan, stiffness, nonlinear, raw, raw_other, more, more_other, edge)

    far_along = send(far, along)

    basis = array(3, GROUP + per_block, slabs, *slab)
    keep, give, sums = pl.pallas_call(
        partner_kernel,
        out_shape=(basis, basis, array(n_space, 8, nz)),
        in_specs=[sm] + [vm] * 10,
        out_specs=(vm,) * 3,
        scratch_shapes=[
            pltpu.VMEM((per_block, WINDOW) + padded, f32),
            pltpu.VMEM((per_block, WINDOW) + slab, modes.dtype),
            pltpu.VMEM((per_block, WINDOW - 2) + slab, f32),
            *field_scratch,
        ],
        compiler_params=pltpu.CompilerParams(vmem_limit_bytes=24 << 20),
        cost_estimate=pl.CostEstimate(flops=40_000_000, bytes_accessed=16 << 20, transcendentals=0),
        name="partner",
    )(plan, near, far, far_along, lap_own, dinv, diag, faces, moments, keep_own, give_own)

    got = send(give, partner_core)
    gathered = lax.all_to_all(sums, "space", 0, 0)

    out = pl.pallas_call(
        combine_kernel,
        out_shape=array(fields, slabs, *slab),
        in_specs=[vm] * 3,
        out_specs=pl.BlockSpec(memory_space=pltpu.HBM),
        scratch_shapes=[pltpu.VMEM((fields, slabs) + slab, f32), pltpu.SemaphoreType.DMA((fields,))],
        compiler_params=pltpu.CompilerParams(vmem_limit_bytes=16 << 20),
        name="combine",
    )(gathered, keep, got)
    return out.reshape((per_block, PARTNERS, slabs, ny, nz))


def solution(mesh):
    return jax.shard_map(
        shards,
        mesh=mesh,
        in_specs=(
            P("mode", "space", None, None),
            P("space", None, None),
            P(),
            P(),
            P("mode", None),
        ),
        out_specs=P("mode", None, "space", None, None),
        check_vma=False,
    )
```
